256 devices in a mesh: gx: 32 (over y, z), gy: 8 (over x, core).
Axes of the slice: x: 4, y: 4, z: 8, core: 2. Of those that a mesh axis runs over, the one named last changes fastest.
Arguments:
- right_sides: bfloat16 [64, 32, 8, 256], P('gx', 'gy'), may hold values from -6 to 6
- leaf_order: int32 [64, 32, 256], P('gx', 'gy'), may hold values from 0 to 255, each once within a row
- leaf_basis: bfloat16 [64, 32, 64, 256], P('gx', 'gy'), may hold values from -0.375 to 0.375
- near_blocks: bfloat16 [64, 32, 256, 2304], P('gx', 'gy'), may hold values from -0.125 to 0.125
- leaf_coupling: bfloat16 [64, 32, 64, 1728], P('gx', 'gy'), may hold values from -0.15625 to 0.15625
- leaf_transfer: bfloat16 [64, 32, 64, 64], P('gx', 'gy'), may hold values from -0.5 to 0.5
- box_coupling: bfloat16 [32, 16, 64, 1728], P('gx', 'gy'), may hold values from -0.15625 to 0.15625
- box_transfer: bfloat16 [32, 16, 64, 64], P('gx', 'gy'), may hold values from -0.5 to 0.5
- coarse_coupling: bfloat16 [32, 8, 64, 4096], P('gx', 'gy'), may hold values from -0.0625 to 0.0625
Outputs:
- product: float32 [64, 32, 8, 256], P('gx', 'gy')
The draws below stay inside these ranges and needn't reach their ends.
Inputs may be any that keep to these rules, and one draw needn't show every extreme that they name: In every leaf, leaf_order names each of 0 to 255 once.
All inputs are finite; a program needn't handle non-finite values.
Results may differ from the reference program's by a relative error of at most 0.0003.
Values may be sent and summed in bfloat16 or wider, within the bound.
A program may use at most 128 MiB of HBM per device.

```python
import jax
import jax.numpy as jnp
import numpy as np
from jax import lax

LEAF = 256
R = 64
RHS = 8
GR = 64
GC = 32
BOX_ROWS = 32
BOX_COLS = 16
COARSE_ROWS = 16
COARSE_COLS = 8
COARSE = 128
HALF = 64
N_GX = 32
N_GY = 8


def shard_levels(key, shape, shards, least, top_value):
    factor_of, own = 1.0, jax.random.fold_in(key, 6)
    for axis_at, blocks in shards:
        steps = jnp.exp(jax.random.uniform(jax.random.fold_in(own, axis_at), (blocks,), jnp.float32, least / len(shards), top_value / len(shards)))
        factor_of = factor_of * jnp.repeat(steps, shape[axis_at] // blocks).reshape([-1 if axis == axis_at else 1 for axis in range(len(shape))])
    return factor_of


def normal_values(stream_key, dims, width, most, cuts=(), kind=jnp.bfloat16):
    entries = jax.random.normal(stream_key, dims, jnp.float32) * width
    if len(cuts) > 0:
        entries = shard_levels(stream_key, dims, cuts, -0.22, 0.18) * entries
    return jnp.clip(entries, min=-most, max=most).astype(kind)


def setup_inputs(seed: int = 0) -> dict:
    seeds = jax.random.split(jax.random.key(seed), 10)
    return {
        "right_sides": normal_values(seeds[0], (GR, GC, RHS, LEAF), 1.0, 6.0, ((0, 32), (1, 8))),
        "leaf_order": jax.vmap(lambda own: jax.random.permutation(own, LEAF))(jax.random.split(seeds[1], GR * GC)).reshape((GR, GC, LEAF)).astype(jnp.int32),
        "leaf_basis": normal_values(seeds[2], (GR, GC, R, LEAF), LEAF ** -0.5, 0.375, ((0, 32), (1, 8))),
        "near_blocks": normal_values(seeds[3], (GR, GC, LEAF, 9 * LEAF), (9 * LEAF) ** -0.5, 0.125, ((0, 32), (1, 8))),
        "leaf_coupling": normal_values(seeds[4], (GR, GC, R, 27 * R), (27 * R) ** -0.5, 0.15625, ((0, 32), (1, 8))),
        "leaf_transfer": normal_values(seeds[5], (GR, GC, R, R), (2 * R) ** -0.5, 0.5, ((0, 32), (1, 8))),
        "box_coupling": normal_values(seeds[6], (BOX_ROWS, BOX_COLS, R, 27 * R), (27 * R) ** -0.5, 0.15625, ((0, 32), (1, 8))),
        "box_transfer": normal_values(seeds[7], (BOX_ROWS, BOX_COLS, R, R), (2 * R) ** -0.5, 0.5, ((0, 32), (1, 8))),
        "coarse_coupling": normal_values(seeds[8], (N_GX, N_GY, R, HALF * R), (COARSE * R) ** -0.5, 0.0625, ((0, 32), (1, 8))),
    }


exact_mode = lax.Precision.HIGHEST


def slot_table():
    chosen_all = np.zeros((2, 2, 27), np.int32)
    for u in range(2):
        for v in range(2):
            chosen = [a * 6 + b for a in range(6) for b in range(6) if max(abs(a - 2 - u), abs(b - 2 - v)) > 1]
            chosen_all[u, v] = np.array(chosen, np.int32)
    return chosen_all


def couple(coeffs, matrices):
    grid_rows = coeffs.shape[0]
    grid_cols = coeffs.shape[1]
    padded = jnp.pad(coeffs, ((2, 2), (2, 2), (0, 0), (0, 0)))
    slots = jnp.asarray(slot_table())

    def one_row(parent):
        first_row = (2 * parent).astype(jnp.int32)
        row_band = lax.dynamic_slice_in_dim(padded, first_row, 6, 0)
        pieces = [row_band[a, b:b + grid_cols:2] for a in range(6) for b in range(6)]
        stacked = jnp.stack(pieces, 0)
        chosen = stacked[slots]
        couplings = lax.dynamic_slice_in_dim(matrices, first_row, 2, 0).astype(jnp.float32)
        couplings = couplings.reshape(2, grid_cols // 2, 2, R, 27, R)
        result = jnp.einsum('uvtqsj,uqvktj->uqvsk', chosen, couplings, precision=exact_mode)
        return result.reshape(2, grid_cols, RHS, R)

    result = lax.map(one_row, jnp.arange(grid_rows // 2, dtype=jnp.int32))
    return result.reshape(grid_rows, grid_cols, RHS, R)


def near_field(ordered, near_blocks):
    grid_rows = ordered.shape[0]
    grid_cols = ordered.shape[1]
    padded = jnp.pad(ordered, ((1, 1), (1, 1), (0, 0), (0, 0)))

    def one_row(row_index):
        row_band = lax.dynamic_slice_in_dim(padded, row_index, 3, 0)
        pieces = [row_band[1 + a, 1 + b:1 + b + grid_cols] for a in (-1, 0, 1) for b in (-1, 0, 1)]
        stacked = jnp.stack(pieces, 1).astype(jnp.float32)
        blocks = lax.dynamic_slice_in_dim(near_blocks, row_index, 1, 0)[0].astype(jnp.float32)
        blocks = blocks.reshape(grid_cols, LEAF, 9, LEAF)
        return jnp.einsum('cqsp,caqp->csa', stacked, blocks, precision=exact_mode)

    return lax.map(one_row, jnp.arange(grid_rows, dtype=jnp.int32))


def coarse_field(coarse_coeffs, coarse_coupling):
    coarse_flat = coarse_coeffs.reshape(COARSE, RHS, R)
    source = jnp.arange(COARSE, dtype=jnp.int32)
    source_row = source // COARSE_COLS
    source_col = source % COARSE_COLS
    target_col = jnp.arange(COARSE_COLS, dtype=jnp.int32)

    def one_row(coarse_row):
        couplings = lax.dynamic_slice_in_dim(coarse_coupling, (2 * coarse_row).astype(jnp.int32), 2, 0).astype(jnp.float32)
        couplings = couplings.reshape(2, COARSE_COLS, R, HALF, R).transpose(1, 2, 0, 3, 4).reshape(COARSE_COLS, R, COARSE, R)
        far_mask = (jnp.abs(source_row[None, :] - coarse_row) > 1) | (jnp.abs(source_col[None, :] - target_col[:, None]) > 1)
        masked = far_mask[:, :, None, None].astype(jnp.float32) * coarse_flat[None]
        return jnp.einsum('jktm,jtsm->jsk', couplings, masked, precision=exact_mode)

    return lax.map(one_row, jnp.arange(COARSE_ROWS, dtype=jnp.int32))


def reference(right_sides, leaf_order, leaf_basis, near_blocks, leaf_coupling, leaf_transfer, box_coupling, box_transfer, coarse_coupling):
    order_index = jnp.broadcast_to(leaf_order[:, :, None, :], right_sides.shape)
    ordered = jnp.take_along_axis(right_sides, order_index, axis=3)
    basis_wide = leaf_basis.astype(jnp.float32)
    leaf_coeffs = jnp.einsum('rcsp,rckp->rcsk', ordered.astype(jnp.float32), basis_wide, precision=exact_mode)
    grouped = leaf_coeffs.reshape(BOX_ROWS, 2, BOX_COLS, 2, RHS, R)
    leaf_up = leaf_transfer.astype(jnp.float32).reshape(BOX_ROWS, 2, BOX_COLS, 2, R, R)
    box_coeffs = jnp.einsum('iujvsk,iujvkm->ijsm', grouped, leaf_up, precision=exact_mode)
    box_up = box_transfer.astype(jnp.float32).reshape(COARSE_ROWS, 2, COARSE_COLS, 2, R, R)
    coarse_coeffs = jnp.einsum('iujvsk,iujvkm->ijsm', box_coeffs.reshape(COARSE_ROWS, 2, COARSE_COLS, 2, RHS, R), box_up, precision=exact_mode)
    coarse_far = coarse_field(coarse_coeffs, coarse_coupling)
    box_far = couple(box_coeffs, box_coupling)
    leaf_far = couple(leaf_coeffs, leaf_coupling)
    coarse_spread = jnp.repeat(jnp.repeat(coarse_far, 2, axis=0), 2, axis=1)
    box_down = jnp.einsum('ijsm,ijkm->ijsk', coarse_spread, box_transfer.astype(jnp.float32), precision=exact_mode) + box_far
    box_spread = jnp.repeat(jnp.repeat(box_down, 2, axis=0), 2, axis=1)
    leaf_down = jnp.einsum('rcsm,rckm->rcsk', box_spread, leaf_transfer.astype(jnp.float32), precision=exact_mode) + leaf_far
    values = jnp.einsum('rcsk,rckp->rcsp', leaf_down, basis_wide, precision=exact_mode) + near_field(ordered, near_blocks)
    inverse = jnp.argsort(leaf_order, axis=-1).astype(jnp.int32)
    inverse_index = jnp.broadcast_to(inverse[:, :, None, :], values.shape)
    return jnp.take_along_axis(values, inverse_index, axis=3)
```

```python
import functools

import jax
import jax.numpy as jnp
from jax import lax
from jax.experimental import pallas as pl
from jax.experimental.pallas import tpu as pltpu
from jax.sharding import PartitionSpec as P

MESH = pl.DeviceIdType.MESH
F32 = jnp.float32
BF16 = jnp.bfloat16


def dot_nt(a, b):
    return lax.dot_general(a, b, (((1,), (1,)), ((), ())), preferred_element_type=F32)


def dot_nn(a, b):
    return lax.dot_general(a, b, (((1,), (0,)), ((), ())), preferred_element_type=F32)


def split(x):
    high = x.astype(BF16).astype(F32)
    return jnp.concatenate([high, x - high], axis=0).astype(BF16)


def joined(out, at=0):
    return out[at : at + 8] + out[at + 8 : at + 16]


def list_positions(u, v):
    return [
        (a, b) for a in range(6) for b in range(6) if max(abs(a - 2 - u), abs(b - 2 - v)) > 1
    ]


def low_lanes(shape):
    return lax.broadcasted_iota(jnp.int32, shape, len(shape) - 1) % 128 < 64


def listed(tiles, swapped, u, v, low):
    where = list_positions(u, v)
    pieces = []
    for i in range(14):
        a, b = where[2 * i]
        first = tiles[a][b // 2] if b % 2 == 0 else swapped[a][b // 2]
        if 2 * i + 1 == len(where):
            pieces.append(first[:, :64])
            continue
        a2, b2 = where[2 * i + 1]
        second = tiles[a2][b2 // 2] if b2 % 2 == 1 else swapped[a2][b2 // 2]
        if first is second:
            pieces.append(first)
        else:
            pieces.append(jnp.where(low, first, second))
    return pieces


def kernel(
    rs_h, order_h, basis_h, near_h, lcp_h, t_h, bcp_h, bt_h, ccp_h,
    out_ref,
    rs, order, basis, near, lcp, tr, bcp, bt, ccp,
    sel, tcat, ohalo, lwin, bwin, pack, row, coarse, half, other_half,
    acc, basis_in,
    load_sem, near_sem,
    p1_send, p1_recv, p2_send, p2_recv,
    o_send, o_recv, l_send, l_recv, b_send, b_recv, x_send, x_recv,
):
    gx = lax.axis_index("gx")
    gy = lax.axis_index("gy")
    y, z = gx // 8, gx % 8
    x, c = gy // 2, gy % 2
    pair, u = gx // 2, gx % 2

    loads = [
        pltpu.make_async_copy(src, dst, load_sem.at[i])
        for i, (src, dst) in enumerate(
            [
                (order_h, order), (rs_h, rs), (basis_h, basis), (t_h, tr), (bt_h, bt),
                (lcp_h, lcp), (bcp_h, bcp), (ccp_h, ccp),
            ]
        )
    ]
    near_loads = [
        pltpu.make_async_copy(near_h.at[i // 4, i % 4], near.at[i], near_sem.at[i])
        for i in range(8)
    ]
    for copy in loads[:5]:
        copy.start()
    for copy in near_loads:
        copy.start()
    for copy in loads[5:]:
        copy.start()

    barrier = pltpu.get_barrier_semaphore()

    def tell(to_gx, to_gy):
        pl.semaphore_signal(barrier, inc=1, device_id=(to_gx, to_gy), device_id_type=MESH)

    own = z * 2 + c
    flip = z + 1 - 2 * (z % 2)
    for d in range(1, 16):
        t = (own + d) % 16
        tell(8 * y + t // 2, 2 * x + t % 2)
    half_id = z % 2
    keeps = y // 2 == half_id
    for j in range(2):
        for dx in range(4):
            from_y = 2 * half_id + (y + j) % 2
            from_z = z if j == 0 else flip
            from_x = (x + 4 - dx) % 4
            if j == 0 and dx == 0:

                @pl.when(jnp.logical_not(keeps))
                def _():
                    tell(8 * from_y + from_z, 2 * from_x + c)
            else:
                tell(8 * from_y + from_z, 2 * from_x + c)
    left, right = (gy + 7) % 8, (gy + 1) % 8
    tell(gx, left)
    tell(gx, right)
    up, down = (gx + 31) % 32, (gx + 1) % 32
    pair_rows = [(pair + 15) % 16, (pair + 1) % 16]
    for other_pair in pair_rows:
        for ut in range(2):
            tell(2 * other_pair + ut, gy)
    partner = 2 * pair + 1 - u
    tell(partner, gy)

    low8 = low_lanes((8, 128))
    low4 = low_lanes((4, 128))

    loads[0].wait()
    loads[1].wait()
    places = lax.broadcasted_iota(jnp.int32, (256, 256), 0)
    ordered = []
    for i in range(8):
        r, k = i // 4, i % 4
        chosen = (places == order[r, k : k + 1, :]).astype(F32).astype(BF16)
        sel[i] = chosen
        points = dot_nn(rs[r, k], chosen)
        ordered.append(points)
        ohalo[1 + r, 1 + k] = points.astype(BF16)
    loads[2].wait()
    tiles = {}
    for r in range(2):
        for w in range(2):
            both = jnp.concatenate([ordered[4 * r + 2 * w], ordered[4 * r + 2 * w + 1]], 0)
            out = dot_nt(both.astype(BF16), basis[r, 2 * w : 2 * w + 2].reshape(128, 256))
            tiles[r, w] = jnp.where(low8, out[:8], out[8:])
            lwin[2 + r, 1 + w] = tiles[r, w]
    loads[3].wait()
    for w in range(2):
        for r in range(2):
            for v in range(2):
                at = (2 * r + v) * 64
                tcat[at : at + 64, 64 * w : 64 * w + 64] = tr[r, 2 * w + v]
    stacked = [split(jnp.concatenate([tiles[0, w], tiles[1, w]], 1)) for w in range(2)]
    out = dot_nn(jnp.concatenate(stacked, 0), tcat[...])
    box = jnp.where(low8, joined(out, 0), joined(out, 16))
    bwin[2 + u, 1] = box
    loads[4].wait()
    bt_all = bt[0].reshape(128, 64)
    part = joined(dot_nn(split(box), jnp.concatenate([bt_all, bt_all], 1)))
    pack[own] = jnp.where(low4, part[:4], part[4:])

    pl.semaphore_wait(barrier, jnp.where(keeps, 29, 30))

    sends = []
    stage1 = []
    for d in range(1, 16):
        t = (own + d) % 16
        copy = pltpu.make_async_remote_copy(
            pack.at[own], pack.at[own], p1_send.at[d - 1], p1_recv.at[d - 1],
            device_id=(8 * y + t // 2, 2 * x + t % 2), device_id_type=MESH,
        )
        copy.start()
        stage1.append(copy)
    column = []

    def send(group, src, dst, ssem, rsem, to):
        copy = pltpu.make_async_remote_copy(
            src, dst, ssem, rsem, device_id=to, device_id_type=MESH
        )
        copy.start()
        group.append(copy)

    own_rows = pl.ds(1, 2)
    send(column, ohalo.at[own_rows, 4], ohalo.at[own_rows, 0], o_send.at[0], o_recv.at[0], (gx, right))
    send(column, ohalo.at[own_rows, 1], ohalo.at[own_rows, 5], o_send.at[1], o_recv.at[1], (gx, left))
    mid = pl.ds(2, 2)
    send(column, lwin.at[mid, 2], lwin.at[mid, 0], l_send.at[0], l_recv.at[0], (gx, right))
    send(column, lwin.at[mid, 1], lwin.at[mid, 3], l_send.at[1], l_recv.at[1], (gx, left))
    send(column, bwin.at[2 + u, 1], bwin.at[2 + u, 0], b_send.at[0], b_recv.at[6], (gx, right))
    send(column, bwin.at[2 + u, 1], bwin.at[2 + u, 2], b_send.at[1], b_recv.at[7], (gx, left))

    def near_terms(i, inside):
        r, k = i // 4, i % 4
        total = None
        for a in (-1, 0, 1):
            for b in (-1, 0, 1):
                if (0 <= r + a < 2 and 0 <= k + b < 4) != inside:
                    continue
                q = 3 * (a + 1) + b + 1
                term = dot_nt(
                    ohalo[1 + r + a, 1 + k + b], near[i, :, q * 256 : (q + 1) * 256]
                )
                total = term if total is None else total + term
        return total

    for i in range(4):
        near_loads[i].wait()
        acc[i] = near_terms(i, True)

    for copy in stage1:
        copy.wait_recv()
    for zp in range(4):
        pairs = [pack[4 * zp + k] + pack[4 * zp + 2 + k] for k in range(2)]
        turned = [pltpu.roll(p, 64, 1) for p in pairs]
        row[zp] = jnp.concatenate(
            [jnp.where(low4, pairs[0], turned[1]), jnp.where(low4, turned[0], pairs[1])], 0
        )
    my_half = y // 2
    odd = jnp.where(z % 2 == my_half, 0, 1)
    to_z = z + odd * (1 - 2 * (z % 2))
    slot = (y % 2) * 4 + x
    stage2 = []
    for i in range(2):
        for dx in range(4):
            to_y = (y + 2 * i + odd) % 4
            to_x = (x + dx) % 4
            copy = pltpu.make_async_remote_copy(
                row, coarse.at[pl.ds((y % 2) * 4, 4), x],
                p2_send.at[4 * i + dx], p2_recv.at[slot],
                device_id=(8 * to_y + to_z, 2 * to_x + c), device_id_type=MESH,
            )
            stage2.append(copy)
            if i == 0 and dx == 0:

                @pl.when(odd == 1)
                def _():
                    copy.start()

                @pl.when(odd == 0)
                def _():
                    pltpu.make_async_copy(
                        row, coarse.at[pl.ds((y % 2) * 4, 4), x], p2_recv.at[slot]
                    ).start()
            else:
                copy.start()

    for copy in column:
        copy.wait()

    @pl.when(gy == 0)
    def _():
        ohalo[1:3, 0] = jnp.zeros((2, 8, 256), BF16)
        lwin[2:4, 0] = jnp.zeros((2, 8, 128), F32)
        bwin[2 + u, 0] = jnp.zeros((8, 128), F32)

    @pl.when(gy == 7)
    def _():
        ohalo[1:3, 5] = jnp.zeros((2, 8, 256), BF16)
        lwin[2:4, 3] = jnp.zeros((2, 8, 128), F32)
        bwin[2 + u, 2] = jnp.zeros((8, 128), F32)

    rows = []
    send(rows, ohalo.at[2], ohalo.at[0], o_send.at[2], o_recv.at[2], (down, gy))
    send(rows, ohalo.at[1], ohalo.at[3], o_send.at[3], o_recv.at[3], (up, gy))
    send(rows, lwin.at[mid], lwin.at[pl.ds(0, 2)], l_send.at[2], l_recv.at[2], (down, gy))
    send(rows, lwin.at[mid], lwin.at[pl.ds(4, 2)], l_send.at[3], l_recv.at[3], (up, gy))
    box_rows = []
    for which, base in ((0, 4), (1, 0)):
        for ut in range(2):
            send(
                box_rows, bwin.at[2 + u], bwin.at[base + u],
                b_send.at[2 + 2 * which + ut], b_recv.at[base + u],
                (2 * pair_rows[which] + ut, gy),
            )
    send(
        box_rows, bwin.at[2 + u], bwin.at[2 + u], b_send.at[6], b_recv.at[2 + u], (partner, gy)
    )

    for i in range(4, 8):
        near_loads[i].wait()
        acc[i] = near_terms(i, True)

    for copy in rows:
        copy.wait()
    for a in (0, 1, 4, 5):
        pltpu.make_async_copy(bwin.at[a], bwin.at[a], b_recv.at[a]).wait()
    pltpu.make_async_copy(bwin.at[3 - u], bwin.at[3 - u], b_recv.at[3 - u]).wait()
    for copy in box_rows:
        copy.wait_send()

    @pl.when(gx == 0)
    def _():
        ohalo[0] = jnp.zeros((6, 8, 256), BF16)
        lwin[0:2] = jnp.zeros((2, 4, 8, 128), F32)

    @pl.when(gx == 31)
    def _():
        ohalo[3] = jnp.zeros((6, 8, 256), BF16)
        lwin[4:6] = jnp.zeros((2, 4, 8, 128), F32)

    @pl.when(pair == 0)
    def _():
        bwin[0:2] = jnp.zeros((2, 3, 8, 128), F32)

    @pl.when(pair == 15)
    def _():
        bwin[4:6] = jnp.zeros((2, 3, 8, 128), F32)

    for i in range(8):
        r, k = i // 4, i % 4
        total = acc[i] + near_terms(i, False)
        both = jnp.concatenate([basis[r, k], split(total)], 0)
        moved = dot_nt(both, sel[i])
        basis_in[i] = moved[:64].astype(BF16)
        acc[i] = joined(moved, 64)

    loads[5].wait()
    leaf_tiles = [[lwin[a, j] for j in range(4)] for a in range(6)]
    leaf_turned = [[pltpu.roll(t, 64, 1) for t in line] for line in leaf_tiles]
    leaf_far = {}
    for r in range(2):
        for w in range(2):
            here = [line[w : w + 3] for line in leaf_tiles]
            here_turned = [line[w : w + 3] for line in leaf_turned]
            both = [
                split(jnp.concatenate(listed(here, here_turned, r, v, low8), 1))
                for v in range(2)
            ]
            out = dot_nt(
                jnp.concatenate(both, 0), lcp[r, 2 * w : 2 * w + 2].reshape(128, 1728)
            )
            leaf_far[r, w] = jnp.where(low8, joined(out, 0), joined(out, 16))
    loads[6].wait()
    box_tiles = [[bwin[a, j] for j in range(3)] for a in range(6)]
    box_turned = [[pltpu.roll(t, 64, 1) for t in line] for line in box_tiles]
    both = []
    for v in range(2):
        even = jnp.concatenate(listed(box_tiles, box_turned, 0, v, low8), 1)
        odds = jnp.concatenate(listed(box_tiles, box_turned, 1, v, low8), 1)
        both.append(split(jnp.where(u == 0, even, odds)))
    out = dot_nt(jnp.concatenate(both, 0), bcp[0].reshape(128, 1728))
    box_far = jnp.where(low8, joined(out, 0), joined(out, 16))

    loads[7].wait()
    for i in range(8):
        pltpu.make_async_copy(row, coarse.at[pl.ds(0, 4), 0], p2_recv.at[i]).wait()
    lane = lax.broadcasted_iota(jnp.int32, (8, 128), 1)
    near_cols = []
    for xs in range(4):
        apart = 2 * xs + lane // 64 - gy
        near_cols.append((apart >= -1) & (apart <= 1))
    sources = []
    for i in range(8):
        apart = 8 * half_id + i - pair
        near_row = (apart >= -1) & (apart <= 1)
        for xs in range(4):
            sources.append(jnp.where(near_cols[xs] & near_row, 0.0, coarse[i, xs]))
    mine = joined(dot_nt(split(jnp.concatenate(sources, 1)), ccp[0, 0]))
    half[...] = mine
    swap = pltpu.make_async_remote_copy(
        half, other_half, x_send.at[0], x_recv.at[0], device_id=(partner, gy), device_id_type=MESH
    )
    swap.start()
    for copy in stage1:
        copy.wait_send()
    for n, copy in enumerate(stage2):
        if n == 0:

            @pl.when(odd == 1)
            def _():
                copy.wait_send()
        else:
            copy.wait_send()
    swap.wait()

    coarse_far = mine + other_half[...]
    box_down = joined(dot_nt(split(coarse_far), bt_all)) + box_far
    both = [split(jnp.where(low8, box_down, 0.0)), split(jnp.where(low8, 0.0, box_down))]
    out = dot_nt(jnp.concatenate(both, 0), tcat[...])
    for r in range(2):
        for w in range(2):
            leaf_down = joined(out[:, 128 * r : 128 * r + 128], 16 * w) + leaf_far[r, w]
            both = [split(jnp.where(low8, leaf_down, 0.0)), split(jnp.where(low8, 0.0, leaf_down))]
            i = 4 * r + 2 * w
            last = dot_nn(jnp.concatenate(both, 0), basis_in[i : i + 2].reshape(128, 256))
            for v in range(2):
                out_ref[r, 2 * w + v] = joined(last, 16 * v) + acc[i + v]


def body(rs, order, basis, near, lcp, tr, bcp, bt, ccp):
    hbm = pl.BlockSpec(memory_space=pltpu.HBM)
    dma = pltpu.SemaphoreType.DMA
    return pl.pallas_call(
        kernel,
        out_shape=jax.ShapeDtypeStruct((2, 4, 8, 256), F32),
        in_specs=[hbm] * 9,
        out_specs=pl.BlockSpec(memory_space=pltpu.VMEM),
        scratch_shapes=[
            pltpu.VMEM(rs.shape, BF16),
            pltpu.VMEM(order.shape, jnp.int32),
            pltpu.VMEM(basis.shape, BF16),
            pltpu.VMEM((8, 256, 2304), BF16),
            pltpu.VMEM(lcp.shape, BF16),
            pltpu.VMEM(tr.shape, BF16),
            pltpu.VMEM(bcp.shape, BF16),
            pltpu.VMEM(bt.shape, BF16),
            pltpu.VMEM(ccp.shape, BF16),
            pltpu.VMEM((8, 256, 256), BF16),
            pltpu.VMEM((256, 128), BF16),
            pltpu.VMEM((4, 6, 8, 256), BF16),
            pltpu.VMEM((6, 4, 8, 128), F32),
            pltpu.VMEM((6, 3, 8, 128), F32),
            pltpu.VMEM((16, 4, 128), F32),
            pltpu.VMEM((4, 8, 128), F32),
            pltpu.VMEM((8, 4, 8, 128), F32),
            pltpu.VMEM((8, 64), F32),
            pltpu.VMEM((8, 64), F32),
            pltpu.VMEM((8, 8, 256), F32),
            pltpu.VMEM((8, 64, 256), BF16),
            dma((8,)),
            dma((8,)),
            dma((15,)),
            dma((15,)),
            dma((8,)),
            dma((8,)),
            dma((4,)),
            dma((4,)),
            dma((4,)),
            dma((4,)),
            dma((7,)),
            dma((8,)),
            dma((1,)),
            dma((1,)),
        ],
        compiler_params=pltpu.CompilerParams(
            collective_id=0, has_side_effects=True, vmem_limit_bytes=56 * 2**20
        ),
    )(rs, order, basis, near, lcp, tr, bcp, bt, ccp)


def solution(mesh):
    four = P("gx", "gy", None, None)
    placed = (four, P("gx", "gy", None)) + (four,) * 7
    return jax.shard_map(body, mesh=mesh, in_specs=placed, out_specs=four, check_vma=False)
```

```python
import functools

import jax
import jax.numpy as jnp
from jax import lax
from jax.experimental import pallas as pl
from jax.experimental.pallas import tpu as pltpu
from jax.sharding import PartitionSpec as P

MESH = pl.DeviceIdType.MESH
F32 = jnp.float32
BF16 = jnp.bfloat16


def dot_nt(a, b):
    return lax.dot_general(a, b, (((1,), (1,)), ((), ())), preferred_element_type=F32)


def dot_nn(a, b):
    return lax.dot_general(a, b, (((1,), (0,)), ((), ())), preferred_element_type=F32)


def split(x):
    high = x.astype(BF16).astype(F32)
    return jnp.concatenate([high, x - high], axis=0).astype(BF16)


def joined(out, at=0):
    return out[at : at + 8] + out[at + 8 : at + 16]


def list_positions(u, v):
    return [
        (a, b) for a in range(6) for b in range(6) if max(abs(a - 2 - u), abs(b - 2 - v)) > 1
    ]


def low_lanes(shape):
    return lax.broadcasted_iota(jnp.int32, shape, len(shape) - 1) % 128 < 64


def listed(tiles, swapped, u, v, low):
    where = list_positions(u, v)
    pieces = []
    for i in range(14):
        a, b = where[2 * i]
        first = tiles[a][b // 2] if b % 2 == 0 else swapped[a][b // 2]
        if 2 * i + 1 == len(where):
            pieces.append(first[:, :64])
            continue
        a2, b2 = where[2 * i + 1]
        second = tiles[a2][b2 // 2] if b2 % 2 == 1 else swapped[a2][b2 // 2]
        if first is second:
            pieces.append(first)
        else:
            pieces.append(jnp.where(low, first, second))
    return pieces


def kernel(
    rs_h, order_h, basis_h, near_h, lcp_h, t_h, bcp_h, bt_h, ccp_h,
    out_ref,
    rs, order, basis, near, lcp, tr, bcp, bt, ccp,
    sel, tcat, ohalo, lwin, bwin, pack, row, coarse, half, other_half,
    acc, basis_in,
    load_sem, near_sem,
    p1_send, p1_recv, p2_send, p2_recv,
    o_send, o_recv, l_send, l_recv, b_send, b_recv, x_send, x_recv,
):
    gx = lax.axis_index("gx")
    gy = lax.axis_index("gy")
    y, z = gx // 8, gx % 8
    x, c = gy // 2, gy % 2
    pair, u = gx // 2, gx % 2

    loads = [
        pltpu.make_async_copy(src, dst, load_sem.at[i])
        for i, (src, dst) in enumerate(
            [
                (order_h, order), (rs_h, rs), (basis_h, basis), (t_h, tr), (bt_h, bt),
                (lcp_h, lcp), (bcp_h, bcp), (ccp_h, ccp),
            ]
        )
    ]
    near_loads = [
        pltpu.make_async_copy(near_h.at[i // 4, i % 4], near.at[i], near_sem.at[i])
        for i in range(8)
    ]
    for copy in loads[:5]:
        copy.start()

    barrier = pltpu.get_barrier_semaphore()

    def tell(to_gx, to_gy):
        pl.semaphore_signal(barrier, inc=1, device_id=(to_gx, to_gy), device_id_type=MESH)

    own = z * 2 + c
    flip = z + 1 - 2 * (z % 2)
    half_id = z % 2
    keeps = y // 2 == half_id
    far_first = sorted(range(1, 16), key=lambda d: abs(d - 8))
    for d in far_first:
        t = (own + d) % 16
        tell(8 * y + t // 2, 2 * x + t % 2)
    for dx in (2, 1, 3, 0):
        for j in range(2):
            from_y = 2 * half_id + (y + j) % 2
            from_z = z if j == 0 else flip
            from_x = (x + 4 - dx) % 4
            if j == 0 and dx == 0:

                @pl.when(jnp.logical_not(keeps))
                def _():
                    tell(8 * from_y + from_z, 2 * from_x + c)
            else:
                tell(8 * from_y + from_z, 2 * from_x + c)
    left, right = (gy + 7) % 8, (gy + 1) % 8
    up, down = (gx + 31) % 32, (gx + 1) % 32
    partner = 2 * pair + 1 - u
    targets = []
    for step in (-1, 1, 0):
        for ut in range(2):
            to_gx = partner if step == 0 else 2 * ((pair + 16 + step) % 16) + ut
            if step == 0 and ut == 1:
                continue
            for to_gy, column in ((left, 2), (gy, 1), (right, 0)):
                targets.append((step, to_gx, to_gy, column))
    targets += [(None, gx, left, 2), (None, gx, right, 0)]
    for _, to_gx, to_gy, _ in targets:
        tell(to_gx, to_gy)
    for copy in near_loads:
        copy.start()
    for copy in loads[5:]:
        copy.start()

    low8 = low_lanes((8, 128))
    low4 = low_lanes((4, 128))

    loads[0].wait()
    loads[1].wait()
    places = lax.broadcasted_iota(jnp.int32, (256, 256), 0)
    ordered = []
    for i in range(8):
        r, k = i // 4, i % 4
        chosen = (places == order[r, k : k + 1, :]).astype(F32).astype(BF16)
        sel[i] = chosen
        points = dot_nn(rs[r, k], chosen)
        ordered.append(points)
        ohalo[1 + r, 1 + k] = points.astype(BF16)
    loads[2].wait()
    tiles = {}
    for r in range(2):
        for w in range(2):
            both = jnp.concatenate([ordered[4 * r + 2 * w], ordered[4 * r + 2 * w + 1]], 0)
            out = dot_nt(both.astype(BF16), basis[r, 2 * w : 2 * w + 2].reshape(128, 256))
            tiles[r, w] = jnp.where(low8, out[:8], out[8:])
            lwin[2 + r, 1 + w] = tiles[r, w]
    loads[3].wait()
    for w in range(2):
        for r in range(2):
            for v in range(2):
                at = (2 * r + v) * 64
                tcat[at : at + 64, 64 * w : 64 * w + 64] = tr[r, 2 * w + v]
    stacked = [split(jnp.concatenate([tiles[0, w], tiles[1, w]], 1)) for w in range(2)]
    out = dot_nn(jnp.concatenate(stacked, 0), tcat[...])
    box = jnp.where(low8, joined(out, 0), joined(out, 16))
    bwin[2 + u, 1] = box
    loads[4].wait()
    bt_all = bt[0].reshape(128, 64)
    part = joined(dot_nn(split(box), jnp.concatenate([bt_all, bt_all], 1)))
    pack[own] = jnp.where(low4, part[:4], part[4:])

    pl.semaphore_wait(barrier, jnp.where(keeps, 39, 40))

    sends = []

    def send(src, dst, ssem, rsem, to):
        copy = pltpu.make_async_remote_copy(
            src, dst, ssem, rsem, device_id=to, device_id_type=MESH
        )
        copy.start()
        sends.append(copy)

    for n, d in enumerate(far_first):
        t = (own + d) % 16
        send(
            pack.at[own], pack.at[own], p1_send.at[n], p1_recv.at[0],
            (8 * y + t // 2, 2 * x + t % 2),
        )
    mine, mid, cols = pl.ds(1, 2), pl.ds(2, 2), pl.ds(1, 4)
    above, below, pairs2 = pl.ds(0, 2), pl.ds(4, 2), pl.ds(1, 2)
    for n, (src, dst, rsem, to) in enumerate([
        (ohalo.at[2, cols], ohalo.at[0, cols], 0, (down, gy)),
        (ohalo.at[1, cols], ohalo.at[3, cols], 1, (up, gy)),
        (ohalo.at[2, 4], ohalo.at[0, 0], 0, (down, right)),
        (ohalo.at[2, 1], ohalo.at[0, 5], 0, (down, left)),
        (ohalo.at[1, 4], ohalo.at[3, 0], 1, (up, right)),
        (ohalo.at[1, 1], ohalo.at[3, 5], 1, (up, left)),
        (ohalo.at[mine, 4], ohalo.at[mine, 0], 2, (gx, right)),
        (ohalo.at[mine, 1], ohalo.at[mine, 5], 3, (gx, left)),
    ]):
        send(src, dst, o_send.at[n], o_recv.at[rsem], to)
    for n, (src, dst, rsem, to) in enumerate([
        (lwin.at[mid, pairs2], lwin.at[above, pairs2], 0, (down, gy)),
        (lwin.at[mid, pairs2], lwin.at[below, pairs2], 1, (up, gy)),
        (lwin.at[mid, 2], lwin.at[above, 0], 0, (down, right)),
        (lwin.at[mid, 1], lwin.at[above, 3], 0, (down, left)),
        (lwin.at[mid, 2], lwin.at[below, 0], 1, (up, right)),
        (lwin.at[mid, 1], lwin.at[below, 3], 1, (up, left)),
        (lwin.at[mid, 2], lwin.at[mid, 0], 2, (gx, right)),
        (lwin.at[mid, 1], lwin.at[mid, 3], 3, (gx, left)),
    ]):
        send(src, dst, l_send.at[n], l_recv.at[rsem], to)
    for n, (step, to_gx, to_gy, column) in enumerate(targets):
        slot = 2 + u if step is None else 2 - 2 * step + u
        send(
            bwin.at[2 + u, 1], bwin.at[slot, column], b_send.at[n], b_recv.at[slot],
            (to_gx, to_gy),
        )

    def near_terms(i, inside):
        r, k = i // 4, i % 4
        total = None
        for a in (-1, 0, 1):
            for b in (-1, 0, 1):
                if (0 <= r + a < 2 and 0 <= k + b < 4) != inside:
                    continue
                q = 3 * (a + 1) + b + 1
                term = dot_nt(
                    ohalo[1 + r + a, 1 + k + b], near[i, :, q * 256 : (q + 1) * 256]
                )
                total = term if total is None else total + term
        return total

    for i in range(8):
        near_loads[i].wait()
        acc[i] = near_terms(i, True)
        basis_in[i] = dot_nt(basis[i // 4, i % 4], sel[i]).astype(BF16)

    arrived = pack.at[pl.ds(0, 15)]
    pltpu.make_async_copy(arrived, arrived, p1_recv.at[0]).wait()
    for zp in range(4):
        pairs = [pack[4 * zp + k] + pack[4 * zp + 2 + k] for k in range(2)]
        turned = [pltpu.roll(p, 64, 1) for p in pairs]
        row[zp] = jnp.concatenate(
            [jnp.where(low4, pairs[0], turned[1]), jnp.where(low4, turned[0], pairs[1])], 0
        )
    my_half = y // 2
    odd = jnp.where(z % 2 == my_half, 0, 1)
    to_z = z + odd * (1 - 2 * (z % 2))
    stage2 = []
    for i in range(2):
        for dx in range(4):
            to_y = (y + 2 * i + odd) % 4
            to_x = (x + dx) % 4
            copy = pltpu.make_async_remote_copy(
                row, coarse.at[pl.ds((y % 2) * 4, 4), x],
                p2_send.at[4 * i + dx], p2_recv.at[0],
                device_id=(8 * to_y + to_z, 2 * to_x + c), device_id_type=MESH,
            )
            stage2.append(copy)
            if i == 0 and dx == 0:

                @pl.when(odd == 1)
                def _():
                    copy.start()

                @pl.when(odd == 0)
                def _():
                    pltpu.make_async_copy(
                        row, coarse.at[pl.ds((y % 2) * 4, 4), x], p2_recv.at[0]
                    ).start()
            else:
                copy.start()

    def arrive(ref, sem):
        pltpu.make_async_copy(ref, ref, sem).wait()

    arrive(ohalo.at[0], o_recv.at[0])
    arrive(ohalo.at[3], o_recv.at[1])
    arrive(ohalo.at[mine, 0], o_recv.at[2])
    arrive(ohalo.at[mine, 5], o_recv.at[3])
    arrive(lwin.at[above], l_recv.at[0])
    arrive(lwin.at[below], l_recv.at[1])
    arrive(lwin.at[mid, 0], l_recv.at[2])
    arrive(lwin.at[mid, 3], l_recv.at[3])
    for a in (0, 1, 4, 5):
        arrive(bwin.at[a], b_recv.at[a])
    arrive(bwin.at[3 - u], b_recv.at[3 - u])
    arrive(bwin.at[2 + u, pl.ds(0, 2)], b_recv.at[2 + u])

    @pl.when(gy == 0)
    def _():
        ohalo[:, 0] = jnp.zeros((4, 8, 256), BF16)
        lwin[:, 0] = jnp.zeros((6, 8, 128), F32)
        bwin[:, 0] = jnp.zeros((6, 8, 128), F32)

    @pl.when(gy == 7)
    def _():
        ohalo[:, 5] = jnp.zeros((4, 8, 256), BF16)
        lwin[:, 3] = jnp.zeros((6, 8, 128), F32)
        bwin[:, 2] = jnp.zeros((6, 8, 128), F32)

    @pl.when(gx == 0)
    def _():
        ohalo[0] = jnp.zeros((6, 8, 256), BF16)
        lwin[0:2] = jnp.zeros((2, 4, 8, 128), F32)

    @pl.when(gx == 31)
    def _():
        ohalo[3] = jnp.zeros((6, 8, 256), BF16)
        lwin[4:6] = jnp.zeros((2, 4, 8, 128), F32)

    @pl.when(pair == 0)
    def _():
        bwin[0:2] = jnp.zeros((2, 3, 8, 128), F32)

    @pl.when(pair == 15)
    def _():
        bwin[4:6] = jnp.zeros((2, 3, 8, 128), F32)

    for i in range(8):
        acc[i] += near_terms(i, False)

    loads[5].wait()
    leaf_tiles = [[lwin[a, j] for j in range(4)] for a in range(6)]
    leaf_turned = [[pltpu.roll(t, 64, 1) for t in line] for line in leaf_tiles]
    leaf_far = {}
    for r in range(2):
        for w in range(2):
            here = [line[w : w + 3] for line in leaf_tiles]
            here_turned = [line[w : w + 3] for line in leaf_turned]
            both = [
                split(jnp.concatenate(listed(here, here_turned, r, v, low8), 1))
                for v in range(2)
            ]
            out = dot_nt(
                jnp.concatenate(both, 0), lcp[r, 2 * w : 2 * w + 2].reshape(128, 1728)
            )
            leaf_far[r, w] = jnp.where(low8, joined(out, 0), joined(out, 16))
    loads[6].wait()
    box_tiles = [[bwin[a, j] for j in range(3)] for a in range(6)]
    box_turned = [[pltpu.roll(t, 64, 1) for t in line] for line in box_tiles]
    both = []
    for v in range(2):
        even = jnp.concatenate(listed(box_tiles, box_turned, 0, v, low8), 1)
        odds = jnp.concatenate(listed(box_tiles, box_turned, 1, v, low8), 1)
        both.append(split(jnp.where(u == 0, even, odds)))
    out = dot_nt(jnp.concatenate(both, 0), bcp[0].reshape(128, 1728))
    box_far = jnp.where(low8, joined(out, 0), joined(out, 16))

    loads[7].wait()
    arrive(coarse, p2_recv.at[0])
    lane = lax.broadcasted_iota(jnp.int32, (8, 128), 1)
    near_cols = []
    for xs in range(4):
        apart = 2 * xs + lane // 64 - gy
        near_cols.append((apart >= -1) & (apart <= 1))
    sources = []
    for i in range(8):
        apart = 8 * half_id + i - pair
        near_row = (apart >= -1) & (apart <= 1)
        for xs in range(4):
            sources.append(jnp.where(near_cols[xs] & near_row, 0.0, coarse[i, xs]))
    here = joined(dot_nt(split(jnp.concatenate(sources, 1)), ccp[0, 0]))
    half[...] = here
    swap = pltpu.make_async_remote_copy(
        half, other_half, x_send.at[0], x_recv.at[0], device_id=(partner, gy), device_id_type=MESH
    )
    swap.start()
    for i in range(8):
        acc[i] = joined(dot_nt(split(acc[i]), sel[i]))
    for copy in sends:
        copy.wait_send()
    for n, copy in enumerate(stage2):
        if n == 0:

            @pl.when(odd == 1)
            def _():
                copy.wait_send()
        else:
            copy.wait_send()
    swap.wait()

    coarse_far = here + other_half[...]
    box_down = joined(dot_nt(split(coarse_far), bt_all)) + box_far
    both = [split(jnp.where(low8, box_down, 0.0)), split(jnp.where(low8, 0.0, box_down))]
    out = dot_nt(jnp.concatenate(both, 0), tcat[...])
    for r in range(2):
        for w in range(2):
            leaf_down = joined(out[:, 128 * r : 128 * r + 128], 16 * w) + leaf_far[r, w]
            both = [split(jnp.where(low8, leaf_down, 0.0)), split(jnp.where(low8, 0.0, leaf_down))]
            i = 4 * r + 2 * w
            last = dot_nn(jnp.concatenate(both, 0), basis_in[i : i + 2].reshape(128, 256))
            for v in range(2):
                out_ref[r, 2 * w + v] = joined(last, 16 * v) + acc[i + v]


def body(rs, order, basis, near, lcp, tr, bcp, bt, ccp):
    hbm = pl.BlockSpec(memory_space=pltpu.HBM)
    dma = pltpu.SemaphoreType.DMA
    return pl.pallas_call(
        kernel,
        out_shape=jax.ShapeDtypeStruct((2, 4, 8, 256), F32),
        in_specs=[hbm] * 9,
        out_specs=pl.BlockSpec(memory_space=pltpu.VMEM),
        scratch_shapes=[
            pltpu.VMEM(rs.shape, BF16),
            pltpu.VMEM(order.shape, jnp.int32),
            pltpu.VMEM(basis.shape, BF16),
            pltpu.VMEM((8, 256, 2304), BF16),
            pltpu.VMEM(lcp.shape, BF16),
            pltpu.VMEM(tr.shape, BF16),
            pltpu.VMEM(bcp.shape, BF16),
            pltpu.VMEM(bt.shape, BF16),
            pltpu.VMEM(ccp.shape, BF16),
            pltpu.VMEM((8, 256, 256), BF16),
            pltpu.VMEM((256, 128), BF16),
            pltpu.VMEM((4, 6, 8, 256), BF16),
            pltpu.VMEM((6, 4, 8, 128), F32),
            pltpu.VMEM((6, 3, 8, 128), F32),
            pltpu.VMEM((16, 4, 128), F32),
            pltpu.VMEM((4, 8, 128), F32),
            pltpu.VMEM((8, 4, 8, 128), F32),
            pltpu.VMEM((8, 64), F32),
            pltpu.VMEM((8, 64), F32),
            pltpu.VMEM((8, 8, 256), F32),
            pltpu.VMEM((8, 64, 256), BF16),
            dma((8,)),
            dma((8,)),
            dma((15,)),
            dma((1,)),
            dma((8,)),
            dma((1,)),
            dma((8,)),
            dma((4,)),
            dma((8,)),
            dma((4,)),
            dma((17,)),
            dma((6,)),
            dma((1,)),
            dma((1,)),
        ],
        compiler_params=pltpu.CompilerParams(
            collective_id=0, has_side_effects=True, vmem_limit_bytes=56 * 2**20
        ),
    )(rs, order, basis, near, lcp, tr, bcp, bt, ccp)


def solution(mesh):
    four = P("gx", "gy", None, None)
    placed = (four, P("gx", "gy", None)) + (four,) * 7
    return jax.shard_map(body, mesh=mesh, in_specs=placed, out_specs=four, check_vma=False)
```

```python
import functools

import jax
import jax.numpy as jnp
from jax import lax
from jax.experimental import pallas as pl
from jax.experimental.pallas import tpu as pltpu
from jax.sharding import PartitionSpec as P

MESH = pl.DeviceIdType.MESH
F32 = jnp.float32
BF16 = jnp.bfloat16


def dot_nt(a, b):
    return lax.dot_general(a, b, (((1,), (1,)), ((), ())), preferred_element_type=F32)


def dot_nn(a, b):
    return lax.dot_general(a, b, (((1,), (0,)), ((), ())), preferred_element_type=F32)


def split(x):
    high = x.astype(BF16).astype(F32)
    return jnp.concatenate([high, x - high], axis=0).astype(BF16)


def joined(out, at=0):
    return out[at : at + 8] + out[at + 8 : at + 16]


def list_positions(u, v):
    return [
        (a, b) for a in range(6) for b in range(6) if max(abs(a - 2 - u), abs(b - 2 - v)) > 1
    ]


def low_lanes(shape):
    return lax.broadcasted_iota(jnp.int32, shape, len(shape) - 1) % 128 < 64


def listed(tiles, swapped, u, v, low):
    where = list_positions(u, v)
    pieces = []
    for i in range(14):
        a, b = where[2 * i]
        first = tiles[a][b // 2] if b % 2 == 0 else swapped[a][b // 2]
        if 2 * i + 1 == len(where):
            pieces.append(first[:, :64])
            continue
        a2, b2 = where[2 * i + 1]
        second = tiles[a2][b2 // 2] if b2 % 2 == 1 else swapped[a2][b2 // 2]
        if first is second:
            pieces.append(first)
        else:
            pieces.append(jnp.where(low, first, second))
    return pieces


def kernel(
    rs_h, order_h, basis_h, near_h, lcp_h, t_h, bcp_h, bt_h, ccp_h,
    out_ref,
    rs, order, basis, near, lcp, tr, bcp, bt, ccp,
    sel, tcat, ohalo, lwin, bwin, pack, row, coarse, half, other_half,
    acc, basis_in,
    load_sem, near_sem,
    p1_send, p1_recv, p2_send, p2_recv,
    o_send, o_recv, l_send, l_recv, b_send, b_recv, x_send, x_recv,
):
    gx = lax.axis_index("gx")
    gy = lax.axis_index("gy")
    y, z = gx // 8, gx % 8
    x, c = gy // 2, gy % 2
    pair, u = gx // 2, gx % 2

    loads = [
        pltpu.make_async_copy(src, dst, load_sem.at[i])
        for i, (src, dst) in enumerate(
            [
                (order_h, order), (rs_h, rs), (basis_h, basis), (t_h, tr), (bt_h, bt),
                (lcp_h, lcp), (bcp_h, bcp), (ccp_h, ccp),
            ]
        )
    ]
    near_loads = [
        pltpu.make_async_copy(near_h.at[i // 4, i % 4], near.at[i], near_sem.at[i])
        for i in range(8)
    ]
    for copy in loads[:5]:
        copy.start()

    barrier = pltpu.get_barrier_semaphore()

    def tell(to_gx, to_gy):
        pl.semaphore_signal(barrier, inc=1, device_id=(to_gx, to_gy), device_id_type=MESH)

    own = z * 2 + c
    flip = z + 1 - 2 * (z % 2)
    half_id = z % 2
    keeps = y // 2 == half_id
    far_first = sorted(range(1, 16), key=lambda d: abs(d - 8))
    for d in far_first:
        t = (own + d) % 16
        tell(8 * y + t // 2, 2 * x + t % 2)
    for dx in (2, 1, 3, 0):
        for j in range(2):
            from_y = 2 * half_id + (y + j) % 2
            from_z = z if j == 0 else flip
            from_x = (x + 4 - dx) % 4
            if j == 0 and dx == 0:

                @pl.when(jnp.logical_not(keeps))
                def _():
                    tell(8 * from_y + from_z, 2 * from_x + c)
            else:
                tell(8 * from_y + from_z, 2 * from_x + c)
    left, right = (gy + 7) % 8, (gy + 1) % 8
    up, down = (gx + 31) % 32, (gx + 1) % 32
    partner = 2 * pair + 1 - u
    targets = []
    for step in (-1, 1, 0):
        for ut in range(2):
            to_gx = partner if step == 0 else 2 * ((pair + 16 + step) % 16) + ut
            if step == 0 and ut == 1:
                continue
            for to_gy, column in ((left, 2), (gy, 1), (right, 0)):
                targets.append((step, to_gx, to_gy, column))
    targets += [(None, gx, left, 2), (None, gx, right, 0)]
    for _, to_gx, to_gy, _ in targets:
        tell(to_gx, to_gy)
    for copy in near_loads:
        copy.start()
    for copy in loads[5:]:
        copy.start()

    low8 = low_lanes((8, 128))
    low4 = low_lanes((4, 128))

    loads[0].wait()
    loads[1].wait()
    places = lax.broadcasted_iota(jnp.int32, (256, 256), 0)
    ordered = []
    for i in range(8):
        r, k = i // 4, i % 4
        chosen = (places == order[r, k : k + 1, :]).astype(F32).astype(BF16)
        sel[i] = chosen
        points = dot_nn(rs[r, k], chosen)
        ordered.append(points)
        ohalo[1 + r, 1 + k] = points.astype(BF16)
    loads[2].wait()
    tiles = {}
    for r in range(2):
        for w in range(2):
            both = jnp.concatenate([ordered[4 * r + 2 * w], ordered[4 * r + 2 * w + 1]], 0)
            out = dot_nt(both.astype(BF16), basis[r, 2 * w : 2 * w + 2].reshape(128, 256))
            tiles[r, w] = jnp.where(low8, out[:8], out[8:])
            lwin[2 + r, 1 + w] = tiles[r, w]
    loads[3].wait()
    for w in range(2):
        for r in range(2):
            for v in range(2):
                at = (2 * r + v) * 64
                tcat[at : at + 64, 64 * w : 64 * w + 64] = tr[r, 2 * w + v]
    stacked = [split(jnp.concatenate([tiles[0, w], tiles[1, w]], 1)) for w in range(2)]
    out = dot_nn(jnp.concatenate(stacked, 0), tcat[...])
    box = jnp.where(low8, joined(out, 0), joined(out, 16))
    bwin[2 + u, 1] = box
    loads[4].wait()
    bt_all = bt[0].reshape(128, 64)
    part = joined(dot_nn(split(box), jnp.concatenate([bt_all, bt_all], 1)))
    pack[own] = jnp.where(low4, part[:4], part[4:])

    pl.semaphore_wait(barrier, jnp.where(keeps, 39, 40))

    sends = []

    def send(src, dst, ssem, rsem, to):
        copy = pltpu.make_async_remote_copy(
            src, dst, ssem, rsem, device_id=to, device_id_type=MESH
        )
        copy.start()
        sends.append(copy)

    for n, d in enumerate(far_first):
        t = (own + d) % 16
        send(
            pack.at[own], pack.at[own], p1_send.at[n], p1_recv.at[0],
            (8 * y + t // 2, 2 * x + t % 2),
        )
    mine, mid, cols = pl.ds(1, 2), pl.ds(2, 2), pl.ds(1, 4)
    above, below, pairs2 = pl.ds(0, 2), pl.ds(4, 2), pl.ds(1, 2)
    for n, (src, dst, rsem, to) in enumerate([
        (ohalo.at[2, cols], ohalo.at[0, cols], 0, (down, gy)),
        (ohalo.at[1, cols], ohalo.at[3, cols], 1, (up, gy)),
        (ohalo.at[2, 4], ohalo.at[0, 0], 0, (down, right)),
        (ohalo.at[2, 1], ohalo.at[0, 5], 0, (down, left)),
        (ohalo.at[1, 4], ohalo.at[3, 0], 1, (up, right)),
        (ohalo.at[1, 1], ohalo.at[3, 5], 1, (up, left)),
        (ohalo.at[mine, 4], ohalo.at[mine, 0], 2, (gx, right)),
        (ohalo.at[mine, 1], ohalo.at[mine, 5], 3, (gx, left)),
    ]):
        send(src, dst, o_send.at[n], o_recv.at[rsem], to)
    for n, (src, dst, rsem, to) in enumerate([
        (lwin.at[mid, pairs2], lwin.at[above, pairs2], 0, (down, gy)),
        (lwin.at[mid, pairs2], lwin.at[below, pairs2], 1, (up, gy)),
        (lwin.at[mid, 2], lwin.at[above, 0], 0, (down, right)),
        (lwin.at[mid, 1], lwin.at[above, 3], 0, (down, left)),
        (lwin.at[mid, 2], lwin.at[below, 0], 1, (up, right)),
        (lwin.at[mid, 1], lwin.at[below, 3], 1, (up, left)),
        (lwin.at[mid, 2], lwin.at[mid, 0], 2, (gx, right)),
        (lwin.at[mid, 1], lwin.at[mid, 3], 3, (gx, left)),
    ]):
        send(src, dst, l_send.at[n], l_recv.at[rsem], to)
    for n, (step, to_gx, to_gy, column) in enumerate(targets):
        slot = 2 + u if step is None else 2 - 2 * step + u
        send(
            bwin.at[2 + u, 1], bwin.at[slot, column], b_send.at[n], b_recv.at[slot],
            (to_gx, to_gy),
        )

    def near_terms(i, inside):
        r, k = i // 4, i % 4
        total = None
        for a in (-1, 0, 1):
            for b in (-1, 0, 1):
                if (0 <= r + a < 2 and 0 <= k + b < 4) != inside:
                    continue
                q = 3 * (a + 1) + b + 1
                term = dot_nt(
                    ohalo[1 + r + a, 1 + k + b], near[i, :, q * 256 : (q + 1) * 256]
                )
                total = term if total is None else total + term
        return total

    for i in range(8):
        near_loads[i].wait()
        acc[i] = near_terms(i, True)
        basis_in[i] = dot_nt(basis[i // 4, i % 4], sel[i]).astype(BF16)

    arrived = pack.at[pl.ds(0, 15)]
    pltpu.make_async_copy(arrived, arrived, p1_recv.at[0]).wait()
    for zp in range(4):
        pairs = [pack[4 * zp + k] + pack[4 * zp + 2 + k] for k in range(2)]
        turned = [pltpu.roll(p, 64, 1) for p in pairs]
        row[zp] = jnp.concatenate(
            [jnp.where(low4, pairs[0], turned[1]), jnp.where(low4, turned[0], pairs[1])], 0
        )
    my_half = y // 2
    odd = jnp.where(z % 2 == my_half, 0, 1)
    to_z = z + odd * (1 - 2 * (z % 2))
    stage2 = []
    for i in range(2):
        for dx in range(4):
            to_y = (y + 2 * i + odd) % 4
            to_x = (x + dx) % 4
            copy = pltpu.make_async_remote_copy(
                row, coarse.at[pl.ds((y % 2) * 4, 4), x],
                p2_send.at[4 * i + dx], p2_recv.at[0],
                device_id=(8 * to_y + to_z, 2 * to_x + c), device_id_type=MESH,
            )
            stage2.append(copy)
            if i == 0 and dx == 0:

                @pl.when(odd == 1)
                def _():
                    copy.start()

                @pl.when(odd == 0)
                def _():
                    pltpu.make_async_copy(
                        row, coarse.at[pl.ds((y % 2) * 4, 4), x], p2_recv.at[0]
                    ).start()
            else:
                copy.start()

    def arrive(ref, sem):
        pltpu.make_async_copy(ref, ref, sem).wait()

    arrive(ohalo.at[0], o_recv.at[0])
    arrive(ohalo.at[3], o_recv.at[1])
    arrive(ohalo.at[mine, 0], o_recv.at[2])
    arrive(ohalo.at[mine, 5], o_recv.at[3])
    arrive(lwin.at[above], l_recv.at[0])
    arrive(lwin.at[below], l_recv.at[1])
    arrive(lwin.at[mid, 0], l_recv.at[2])
    arrive(lwin.at[mid, 3], l_recv.at[3])
    for a in (0, 1, 4, 5):
        arrive(bwin.at[a], b_recv.at[a])
    arrive(bwin.at[3 - u], b_recv.at[3 - u])
    arrive(bwin.at[2 + u, pl.ds(0, 2)], b_recv.at[2 + u])

    @pl.when(gy == 0)
    def _():
        ohalo[:, 0] = jnp.zeros((4, 8, 256), BF16)
        lwin[:, 0] = jnp.zeros((6, 8, 128), F32)
        bwin[:, 0] = jnp.zeros((6, 8, 128), F32)

    @pl.when(gy == 7)
    def _():
        ohalo[:, 5] = jnp.zeros((4, 8, 256), BF16)
        lwin[:, 3] = jnp.zeros((6, 8, 128), F32)
        bwin[:, 2] = jnp.zeros((6, 8, 128), F32)

    @pl.when(gx == 0)
    def _():
        ohalo[0] = jnp.zeros((6, 8, 256), BF16)
        lwin[0:2] = jnp.zeros((2, 4, 8, 128), F32)

    @pl.when(gx == 31)
    def _():
        ohalo[3] = jnp.zeros((6, 8, 256), BF16)
        lwin[4:6] = jnp.zeros((2, 4, 8, 128), F32)

    @pl.when(pair == 0)
    def _():
        bwin[0:2] = jnp.zeros((2, 3, 8, 128), F32)

    @pl.when(pair == 15)
    def _():
        bwin[4:6] = jnp.zeros((2, 3, 8, 128), F32)

    for i in range(8):
        acc[i] += near_terms(i, False)

    loads[5].wait()
    leaf_tiles = [[lwin[a, j] for j in range(4)] for a in range(6)]
    leaf_turned = [[pltpu.roll(t, 64, 1) for t in line] for line in leaf_tiles]
    leaf_far = {}
    for r in range(2):
        for w in range(2):
            here = [line[w : w + 3] for line in leaf_tiles]
            here_turned = [line[w : w + 3] for line in leaf_turned]
            both = [
                split(jnp.concatenate(listed(here, here_turned, r, v, low8), 1))
                for v in range(2)
            ]
            out = dot_nt(
                jnp.concatenate(both, 0), lcp[r, 2 * w : 2 * w + 2].reshape(128, 1728)
            )
            leaf_far[r, w] = jnp.where(low8, joined(out, 0), joined(out, 16))
    loads[6].wait()
    box_tiles = [[bwin[a, j] for j in range(3)] for a in range(6)]
    box_turned = [[pltpu.roll(t, 64, 1) for t in line] for line in box_tiles]
    both = []
    for v in range(2):
        even = jnp.concatenate(listed(box_tiles, box_turned, 0, v, low8), 1)
        odds = jnp.concatenate(listed(box_tiles, box_turned, 1, v, low8), 1)
        both.append(split(jnp.where(u == 0, even, odds)))
    out = dot_nt(jnp.concatenate(both, 0), bcp[0].reshape(128, 1728))
    box_far = jnp.where(low8, joined(out, 0), joined(out, 16))

    loads[7].wait()
    arrive(coarse, p2_recv.at[0])
    lane = lax.broadcasted_iota(jnp.int32, (8, 128), 1)
    near_cols = []
    for xs in range(4):
        apart = 2 * xs + lane // 64 - gy
        near_cols.append((apart >= -1) & (apart <= 1))
    sources = []
    for i in range(8):
        apart = 8 * half_id + i - pair
        near_row = (apart >= -1) & (apart <= 1)
        for xs in range(4):
            sources.append(jnp.where(near_cols[xs] & near_row, 0.0, coarse[i, xs]))
    here = joined(dot_nt(split(jnp.concatenate(sources, 1)), ccp[0, 0]))
    half[...] = here
    swap = pltpu.make_async_remote_copy(
        half, other_half, x_send.at[0], x_recv.at[0], device_id=(partner, gy), device_id_type=MESH
    )
    swap.start()
    for i in range(8):
        acc[i] = joined(dot_nt(split(acc[i]), sel[i]))
    for copy in sends:
        copy.wait_send()
    for n, copy in enumerate(stage2):
        if n == 0:

            @pl.when(odd == 1)
            def _():
                copy.wait_send()
        else:
            copy.wait_send()
    swap.wait()

    coarse_far = here + other_half[...]
    box_down = joined(dot_nt(split(coarse_far), bt_all)) + box_far
    both = [split(jnp.where(low8, box_down, 0.0)), split(jnp.where(low8, 0.0, box_down))]
    out = dot_nt(jnp.concatenate(both, 0), tcat[...])
    for r in range(2):
        for w in range(2):
            leaf_down = joined(out[:, 128 * r : 128 * r + 128], 16 * w) + leaf_far[r, w]
            both = [split(jnp.where(low8, leaf_down, 0.0)), split(jnp.where(low8, 0.0, leaf_down))]
            i = 4 * r + 2 * w
            last = dot_nn(jnp.concatenate(both, 0), basis_in[i : i + 2].reshape(128, 256))
            for v in range(2):
                out_ref[r, 2 * w + v] = joined(last, 16 * v) + acc[i + v]


def body(*args):
    rs, order, basis, _, lcp, tr, bcp, bt, ccp = args
    hbm = pl.BlockSpec(memory_space=pltpu.HBM)
    dma = pltpu.SemaphoreType.DMA
    return pl.pallas_call(
        kernel,
        out_shape=jax.ShapeDtypeStruct((2, 4, 8, 256), F32),
        in_specs=[hbm] * 9,
        out_specs=pl.BlockSpec(memory_space=pltpu.VMEM),
        scratch_shapes=[
            pltpu.VMEM(rs.shape, BF16),
            pltpu.VMEM(order.shape, jnp.int32),
            pltpu.VMEM(basis.shape, BF16),
            pltpu.VMEM((8, 256, 2304), BF16),
            pltpu.VMEM(lcp.shape, BF16),
            pltpu.VMEM(tr.shape, BF16),
            pltpu.VMEM(bcp.shape, BF16),
            pltpu.VMEM(bt.shape, BF16),
            pltpu.VMEM(ccp.shape, BF16),
            pltpu.VMEM((8, 256, 256), BF16),
            pltpu.VMEM((256, 128), BF16),
            pltpu.VMEM((4, 6, 8, 256), BF16),
            pltpu.VMEM((6, 4, 8, 128), F32),
            pltpu.VMEM((6, 3, 8, 128), F32),
            pltpu.VMEM((16, 4, 128), F32),
            pltpu.VMEM((4, 8, 128), F32),
            pltpu.VMEM((8, 4, 8, 128), F32),
            pltpu.VMEM((8, 64), F32),
            pltpu.VMEM((8, 64), F32),
            pltpu.VMEM((8, 8, 256), F32),
            pltpu.VMEM((8, 64, 256), BF16),
            dma((8,)),
            dma((8,)),
            dma((15,)),
            dma((1,)),
            dma((8,)),
            dma((1,)),
            dma((8,)),
            dma((4,)),
            dma((8,)),
            dma((4,)),
            dma((17,)),
            dma((6,)),
            dma((1,)),
            dma((1,)),
        ],
        compiler_params=pltpu.CompilerParams(
            collective_id=0, has_side_effects=True, vmem_limit_bytes=40 * 2**20
        ),
    )(*(pltpu.with_memory_space_constraint(v, pltpu.HBM) for v in args))


def solution(mesh):
    four = P("gx", "gy", None, None)
    placed = (four, P("gx", "gy", None)) + (four,) * 7
    return jax.shard_map(body, mesh=mesh, in_specs=placed, out_specs=four, check_vma=False)
```

```python
import functools

import jax
import jax.numpy as jnp
from jax import lax
from jax.experimental import pallas as pl
from jax.experimental.pallas import tpu as pltpu
from jax.sharding import PartitionSpec as P

MESH = pl.DeviceIdType.MESH
F32 = jnp.float32
BF16 = jnp.bfloat16


def dot_nt(a, b):
    return lax.dot_general(a, b, (((1,), (1,)), ((), ())), preferred_element_type=F32)


def dot_nn(a, b):
    return lax.dot_general(a, b, (((1,), (0,)), ((), ())), preferred_element_type=F32)


def split(x):
    high = x.astype(BF16).astype(F32)
    return jnp.concatenate([high, x - high], axis=0).astype(BF16)


def joined(out, at=0):
    return out[at : at + 8] + out[at + 8 : at + 16]


def list_positions(u, v):
    return [
        (a, b) for a in range(6) for b in range(6) if max(abs(a - 2 - u), abs(b - 2 - v)) > 1
    ]


def low_lanes(shape):
    return lax.broadcasted_iota(jnp.int32, shape, len(shape) - 1) % 128 < 64


def listed(tiles, swapped, u, v, low):
    where = list_positions(u, v)
    pieces = []
    for i in range(14):
        a, b = where[2 * i]
        first = tiles[a][b // 2] if b % 2 == 0 else swapped[a][b // 2]
        if 2 * i + 1 == len(where):
            pieces.append(first[:, :64])
            continue
        a2, b2 = where[2 * i + 1]
        second = tiles[a2][b2 // 2] if b2 % 2 == 1 else swapped[a2][b2 // 2]
        if first is second:
            pieces.append(first)
        else:
            pieces.append(jnp.where(low, first, second))
    return pieces


def kernel(
    rs_h, order_h, basis_h, near_h, lcp_h, t_h, bcp_h, bt_h, ccp_h,
    out_ref,
    rs, order, basis, near, lcp, tr, bcp, bt, ccp,
    sel, tcat, ohalo, lwin, bwin, pack, row, coarse, half, other_half,
    acc, basis_in,
    load_sem, near_sem,
    p1_send, p1_recv, p2_send, p2_recv,
    o_send, o_recv, l_send, l_recv, b_send, b_recv, x_send, x_recv,
):
    gx = lax.axis_index("gx")
    gy = lax.axis_index("gy")
    y, z = gx // 8, gx % 8
    x, c = gy // 2, gy % 2
    pair, u = gx // 2, gx % 2

    loads = [
        pltpu.make_async_copy(src, dst, load_sem.at[i])
        for i, (src, dst) in enumerate(
            [
                (order_h, order), (rs_h, rs), (basis_h, basis), (t_h, tr), (bt_h, bt),
                (lcp_h, lcp), (bcp_h, bcp), (ccp_h, ccp),
            ]
        )
    ]
    near_loads = [
        pltpu.make_async_copy(near_h.at[i // 4, i % 4], near.at[i], near_sem.at[i])
        for i in range(8)
    ]
    for copy in loads[:5]:
        copy.start()

    barrier = pltpu.get_barrier_semaphore()

    def tell(to_gx, to_gy):
        pl.semaphore_signal(barrier, inc=1, device_id=(to_gx, to_gy), device_id_type=MESH)

    own = z * 2 + c
    flip = z + 1 - 2 * (z % 2)
    half_id = z % 2
    keeps = y // 2 == half_id
    far_first = sorted(range(1, 16), key=lambda d: abs(d - 8))
    for d in far_first:
        t = (own + d) % 16
        tell(8 * y + t // 2, 2 * x + t % 2)
    for dx in (2, 1, 3, 0):
        for j in range(2):
            from_y = 2 * half_id + (y + j) % 2
            from_z = z if j == 0 else flip
            from_x = (x + 4 - dx) % 4
            if j == 0 and dx == 0:

                @pl.when(jnp.logical_not(keeps))
                def _():
                    tell(8 * from_y + from_z, 2 * from_x + c)
            else:
                tell(8 * from_y + from_z, 2 * from_x + c)
    left, right = (gy + 7) % 8, (gy + 1) % 8
    up, down = (gx + 31) % 32, (gx + 1) % 32
    partner = 2 * pair + 1 - u
    targets = []
    for step in (-1, 1, 0):
        for ut in range(2):
            to_gx = partner if step == 0 else 2 * ((pair + 16 + step) % 16) + ut
            if step == 0 and ut == 1:
                continue
            for to_gy, column in ((left, 2), (gy, 1), (right, 0)):
                targets.append((step, to_gx, to_gy, column))
    targets += [(None, gx, left, 2), (None, gx, right, 0)]
    for _, to_gx, to_gy, _ in targets:
        tell(to_gx, to_gy)
    for copy in near_loads:
        copy.start()
    for copy in loads[5:]:
        copy.start()

    low8 = low_lanes((8, 128))
    low4 = low_lanes((4, 128))

    loads[0].wait()
    loads[1].wait()
    places = lax.broadcasted_iota(jnp.int32, (256, 256), 0)
    ordered = []
    for i in range(8):
        r, k = i // 4, i % 4
        chosen = (places == order[r, k : k + 1, :]).astype(F32).astype(BF16)
        sel[i] = chosen
        points = dot_nn(rs[r, k], chosen)
        ordered.append(points)
        ohalo[1 + r, 1 + k] = points.astype(BF16)
    loads[2].wait()
    tiles = {}
    for r in range(2):
        for w in range(2):
            both = jnp.concatenate([ordered[4 * r + 2 * w], ordered[4 * r + 2 * w + 1]], 0)
            out = dot_nt(both.astype(BF16), basis[r, 2 * w : 2 * w + 2].reshape(128, 256))
            tiles[r, w] = jnp.where(low8, out[:8], out[8:])
            lwin[2 + r, 1 + w] = tiles[r, w]
    loads[3].wait()
    for w in range(2):
        for r in range(2):
            for v in range(2):
                at = (2 * r + v) * 64
                tcat[at : at + 64, 64 * w : 64 * w + 64] = tr[r, 2 * w + v]
    stacked = [split(jnp.concatenate([tiles[0, w], tiles[1, w]], 1)) for w in range(2)]
    out = dot_nn(jnp.concatenate(stacked, 0), tcat[...])
    box = jnp.where(low8, joined(out, 0), joined(out, 16))
    bwin[2 + u, 1] = box
    loads[4].wait()
    bt_all = bt[0].reshape(128, 64)
    part = joined(dot_nn(split(box), jnp.concatenate([bt_all, bt_all], 1)))
    pack[own] = jnp.where(low4, part[:4], part[4:])

    pl.semaphore_wait(barrier, jnp.where(keeps, 39, 40))

    sends = []

    def send(src, dst, ssem, rsem, to):
        copy = pltpu.make_async_remote_copy(
            src, dst, ssem, rsem, device_id=to, device_id_type=MESH
        )
        copy.start()
        sends.append(copy)

    for n, d in enumerate(far_first):
        t = (own + d) % 16
        send(
            pack.at[own], pack.at[own], p1_send.at[n], p1_recv.at[0],
            (8 * y + t // 2, 2 * x + t % 2),
        )
    mine, mid, cols = pl.ds(1, 2), pl.ds(2, 2), pl.ds(1, 4)
    above, below, pairs2 = pl.ds(0, 2), pl.ds(4, 2), pl.ds(1, 2)
    for n, (src, dst, rsem, to) in enumerate([
        (ohalo.at[2, cols], ohalo.at[0, cols], 0, (down, gy)),
        (ohalo.at[1, cols], ohalo.at[3, cols], 1, (up, gy)),
        (ohalo.at[2, 4], ohalo.at[0, 0], 0, (down, right)),
        (ohalo.at[2, 1], ohalo.at[0, 5], 0, (down, left)),
        (ohalo.at[1, 4], ohalo.at[3, 0], 1, (up, right)),
        (ohalo.at[1, 1], ohalo.at[3, 5], 1, (up, left)),
        (ohalo.at[mine, 4], ohalo.at[mine, 0], 2, (gx, right)),
        (ohalo.at[mine, 1], ohalo.at[mine, 5], 3, (gx, left)),
    ]):
        send(src, dst, o_send.at[n], o_recv.at[rsem], to)
    for n, (src, dst, rsem, to) in enumerate([
        (lwin.at[mid, pairs2], lwin.at[above, pairs2], 0, (down, gy)),
        (lwin.at[mid, pairs2], lwin.at[below, pairs2], 1, (up, gy)),
        (lwin.at[mid, 2], lwin.at[above, 0], 0, (down, right)),
        (lwin.at[mid, 1], lwin.at[above, 3], 0, (down, left)),
        (lwin.at[mid, 2], lwin.at[below, 0], 1, (up, right)),
        (lwin.at[mid, 1], lwin.at[below, 3], 1, (up, left)),
        (lwin.at[mid, 2], lwin.at[mid, 0], 2, (gx, right)),
        (lwin.at[mid, 1], lwin.at[mid, 3], 3, (gx, left)),
    ]):
        send(src, dst, l_send.at[n], l_recv.at[rsem], to)
    for n, (step, to_gx, to_gy, column) in enumerate(targets):
        slot = 2 + u if step is None else 2 - 2 * step + u
        send(
            bwin.at[2 + u, 1], bwin.at[slot, column], b_send.at[n], b_recv.at[slot],
            (to_gx, to_gy),
        )

    def near_terms(i, inside):
        r, k = i // 4, i % 4
        total = None
        for a in (-1, 0, 1):
            for b in (-1, 0, 1):
                if (0 <= r + a < 2 and 0 <= k + b < 4) != inside:
                    continue
                q = 3 * (a + 1) + b + 1
                term = dot_nt(
                    ohalo[1 + r + a, 1 + k + b], near[i, :, q * 256 : (q + 1) * 256]
                )
                total = term if total is None else total + term
        return total

    for i in range(8):
        near_loads[i].wait()
        acc[i] = near_terms(i, True)
        basis_in[i] = dot_nt(basis[i // 4, i % 4], sel[i]).astype(BF16)

    arrived = pack.at[pl.ds(0, 15)]
    pltpu.make_async_copy(arrived, arrived, p1_recv.at[0]).wait()
    for zp in range(4):
        pairs = [pack[4 * zp + k] + pack[4 * zp + 2 + k] for k in range(2)]
        turned = [pltpu.roll(p, 64, 1) for p in pairs]
        row[zp] = jnp.concatenate(
            [jnp.where(low4, pairs[0], turned[1]), jnp.where(low4, turned[0], pairs[1])], 0
        )
    my_half = y // 2
    odd = jnp.where(z % 2 == my_half, 0, 1)
    to_z = z + odd * (1 - 2 * (z % 2))
    stage2 = []
    for i in range(2):
        for dx in range(4):
            to_y = (y + 2 * i + odd) % 4
            to_x = (x + dx) % 4
            copy = pltpu.make_async_remote_copy(
                row, coarse.at[(y % 2) * 4 + x],
                p2_send.at[4 * i + dx], p2_recv.at[0],
                device_id=(8 * to_y + to_z, 2 * to_x + c), device_id_type=MESH,
            )
            stage2.append(copy)
            if i == 0 and dx == 0:

                @pl.when(odd == 1)
                def _():
                    copy.start()

                @pl.when(odd == 0)
                def _():
                    pltpu.make_async_copy(
                        row, coarse.at[(y % 2) * 4 + x], p2_recv.at[0]
                    ).start()
            else:
                copy.start()

    def arrive(ref, sem):
        pltpu.make_async_copy(ref, ref, sem).wait()

    arrive(ohalo.at[0], o_recv.at[0])
    arrive(ohalo.at[3], o_recv.at[1])
    arrive(ohalo.at[mine, 0], o_recv.at[2])
    arrive(ohalo.at[mine, 5], o_recv.at[3])
    arrive(lwin.at[above], l_recv.at[0])
    arrive(lwin.at[below], l_recv.at[1])
    arrive(lwin.at[mid, 0], l_recv.at[2])
    arrive(lwin.at[mid, 3], l_recv.at[3])
    for a in (0, 1, 4, 5):
        arrive(bwin.at[a], b_recv.at[a])
    arrive(bwin.at[3 - u], b_recv.at[3 - u])
    arrive(bwin.at[2 + u, pl.ds(0, 2)], b_recv.at[2 + u])

    @pl.when(gy == 0)
    def _():
        ohalo[:, 0] = jnp.zeros((4, 8, 256), BF16)
        lwin[:, 0] = jnp.zeros((6, 8, 128), F32)
        bwin[:, 0] = jnp.zeros((6, 8, 128), F32)

    @pl.when(gy == 7)
    def _():
        ohalo[:, 5] = jnp.zeros((4, 8, 256), BF16)
        lwin[:, 3] = jnp.zeros((6, 8, 128), F32)
        bwin[:, 2] = jnp.zeros((6, 8, 128), F32)

    @pl.when(gx == 0)
    def _():
        ohalo[0] = jnp.zeros((6, 8, 256), BF16)
        lwin[0:2] = jnp.zeros((2, 4, 8, 128), F32)

    @pl.when(gx == 31)
    def _():
        ohalo[3] = jnp.zeros((6, 8, 256), BF16)
        lwin[4:6] = jnp.zeros((2, 4, 8, 128), F32)

    @pl.when(pair == 0)
    def _():
        bwin[0:2] = jnp.zeros((2, 3, 8, 128), F32)

    @pl.when(pair == 15)
    def _():
        bwin[4:6] = jnp.zeros((2, 3, 8, 128), F32)

    for i in range(8):
        acc[i] += near_terms(i, False)

    loads[5].wait()
    leaf_tiles = [[lwin[a, j] for j in range(4)] for a in range(6)]
    leaf_turned = [[pltpu.roll(t, 64, 1) for t in line] for line in leaf_tiles]
    leaf_far = {}
    for r in range(2):
        for w in range(2):
            here = [line[w : w + 3] for line in leaf_tiles]
            here_turned = [line[w : w + 3] for line in leaf_turned]
            both = [
                split(jnp.concatenate(listed(here, here_turned, r, v, low8), 1))
                for v in range(2)
            ]
            out = dot_nt(
                jnp.concatenate(both, 0), lcp[r, 2 * w : 2 * w + 2].reshape(128, 1728)
            )
            leaf_far[r, w] = jnp.where(low8, joined(out, 0), joined(out, 16))
    loads[6].wait()
    box_tiles = [[bwin[a, j] for j in range(3)] for a in range(6)]
    box_turned = [[pltpu.roll(t, 64, 1) for t in line] for line in box_tiles]
    both = []
    for v in range(2):
        even = jnp.concatenate(listed(box_tiles, box_turned, 0, v, low8), 1)
        odds = jnp.concatenate(listed(box_tiles, box_turned, 1, v, low8), 1)
        both.append(split(jnp.where(u == 0, even, odds)))
    out = dot_nt(jnp.concatenate(both, 0), bcp[0].reshape(128, 1728))
    box_far = jnp.where(low8, joined(out, 0), joined(out, 16))

    loads[7].wait()
    arrive(coarse, p2_recv.at[0])
    lane = lax.broadcasted_iota(jnp.int32, (8, 128), 1)
    near_cols = []
    for xs in range(4):
        apart = 2 * xs + lane // 64 - gy
        near_cols.append((apart >= -1) & (apart <= 1))
    sources = []
    for i in range(8):
        apart = 8 * half_id + i - pair
        near_row = (apart >= -1) & (apart <= 1)
        for xs in range(4):
            sources.append(jnp.where(near_cols[xs] & near_row, 0.0, coarse[i // 4 * 4 + xs, i % 4]))
    here = joined(dot_nt(split(jnp.concatenate(sources, 1)), ccp[0, 0]))
    half[...] = here
    swap = pltpu.make_async_remote_copy(
        half, other_half, x_send.at[0], x_recv.at[0], device_id=(partner, gy), device_id_type=MESH
    )
    swap.start()
    for i in range(8):
        acc[i] = joined(dot_nt(split(acc[i]), sel[i]))
    for copy in sends:
        copy.wait_send()
    for n, copy in enumerate(stage2):
        if n == 0:

            @pl.when(odd == 1)
            def _():
                copy.wait_send()
        else:
            copy.wait_send()
    swap.wait()

    coarse_far = here + other_half[...]
    box_down = joined(dot_nt(split(coarse_far), bt_all)) + box_far
    both = [split(jnp.where(low8, box_down, 0.0)), split(jnp.where(low8, 0.0, box_down))]
    out = dot_nt(jnp.concatenate(both, 0), tcat[...])
    for r in range(2):
        for w in range(2):
            leaf_down = joined(out[:, 128 * r : 128 * r + 128], 16 * w) + leaf_far[r, w]
            both = [split(jnp.where(low8, leaf_down, 0.0)), split(jnp.where(low8, 0.0, leaf_down))]
            i = 4 * r + 2 * w
            last = dot_nn(jnp.concatenate(both, 0), basis_in[i : i + 2].reshape(128, 256))
            for v in range(2):
                out_ref[r, 2 * w + v] = joined(last, 16 * v) + acc[i + v]


def body(*args):
    rs, order, basis, _, lcp, tr, bcp, bt, ccp = args
    hbm = pl.BlockSpec(memory_space=pltpu.HBM)
    dma = pltpu.SemaphoreType.DMA
    return pl.pallas_call(
        kernel,
        out_shape=jax.ShapeDtypeStruct((2, 4, 8, 256), F32),
        in_specs=[hbm] * 9,
        out_specs=pl.BlockSpec(memory_space=pltpu.VMEM),
        scratch_shapes=[
            pltpu.VMEM(rs.shape, BF16),
            pltpu.VMEM(order.shape, jnp.int32),
            pltpu.VMEM(basis.shape, BF16),
            pltpu.VMEM((8, 256, 2304), BF16),
            pltpu.VMEM(lcp.shape, BF16),
            pltpu.VMEM(tr.shape, BF16),
            pltpu.VMEM(bcp.shape, BF16),
            pltpu.VMEM(bt.shape, BF16),
            pltpu.VMEM(ccp.shape, BF16),
            pltpu.VMEM((8, 256, 256), BF16),
            pltpu.VMEM((256, 128), BF16),
            pltpu.VMEM((4, 6, 8, 256), BF16),
            pltpu.VMEM((6, 4, 8, 128), F32),
            pltpu.VMEM((6, 3, 8, 128), F32),
            pltpu.VMEM((16, 4, 128), F32),
            pltpu.VMEM((4, 8, 128), F32),
            pltpu.VMEM((8, 4, 8, 128), F32),
            pltpu.VMEM((8, 64), F32),
            pltpu.VMEM((8, 64), F32),
            pltpu.VMEM((8, 8, 256), F32),
            pltpu.VMEM((8, 64, 256), BF16),
            dma((8,)),
            dma((8,)),
            dma((15,)),
            dma((1,)),
            dma((8,)),
            dma((1,)),
            dma((8,)),
            dma((4,)),
            dma((8,)),
            dma((4,)),
            dma((17,)),
            dma((6,)),
            dma((1,)),
            dma((1,)),
        ],
        compiler_params=pltpu.CompilerParams(
            collective_id=0, has_side_effects=True, vmem_limit_bytes=40 * 2**20
        ),
    )(*(pltpu.with_memory_space_constraint(v, pltpu.HBM) for v in args))


def solution(mesh):
    four = P("gx", "gy", None, None)
    placed = (four, P("gx", "gy", None)) + (four,) * 7
    return jax.shard_map(body, mesh=mesh, in_specs=placed, out_specs=four, check_vma=False)
```

```python
import functools

import jax
import jax.numpy as jnp
from jax import lax
from jax.experimental import pallas as pl
from jax.experimental.pallas import tpu as pltpu
from jax.sharding import PartitionSpec as P

MESH = pl.DeviceIdType.MESH
F32 = jnp.float32
BF16 = jnp.bfloat16


def dot_nt(a, b):
    return lax.dot_general(a, b, (((1,), (1,)), ((), ())), preferred_element_type=F32)


def dot_nn(a, b):
    return lax.dot_general(a, b, (((1,), (0,)), ((), ())), preferred_element_type=F32)


def split(x):
    high = x.astype(BF16).astype(F32)
    return jnp.concatenate([high, x - high], axis=0).astype(BF16)


def joined(out, at=0):
    return out[at : at + 8] + out[at + 8 : at + 16]


def list_positions(u, v):
    return [
        (a, b) for a in range(6) for b in range(6) if max(abs(a - 2 - u), abs(b - 2 - v)) > 1
    ]


def low_lanes(shape):
    return lax.broadcasted_iota(jnp.int32, shape, len(shape) - 1) % 128 < 64


def listed(tiles, swapped, u, v, low):
    where = list_positions(u, v)
    pieces = []
    for i in range(14):
        a, b = where[2 * i]
        first = tiles[a][b // 2] if b % 2 == 0 else swapped[a][b // 2]
        if 2 * i + 1 == len(where):
            pieces.append(first[:, :64])
            continue
        a2, b2 = where[2 * i + 1]
        second = tiles[a2][b2 // 2] if b2 % 2 == 1 else swapped[a2][b2 // 2]
        if first is second:
            pieces.append(first)
        else:
            pieces.append(jnp.where(low, first, second))
    return pieces


def kernel(
    rs_h, order_h, basis_h, near_h, lcp_h, t_h, bcp_h, bt_h, ccp_h,
    out_ref,
    rs, order, basis, near, lcp, tr, bcp, bt, ccp,
    sel, tcat, ohalo, lwin, bwin, pack, row, coarse, half, other_half,
    acc, basis_in, through,
    load_sem, near_sem,
    p1_send, p1_recv, p2_send, p2_recv,
    o_send, o_recv, l_send, l_recv, b_send, b_recv, x_send, x_recv,
):
    gx = lax.axis_index("gx")
    gy = lax.axis_index("gy")
    y, z = gx // 8, gx % 8
    x, c = gy // 2, gy % 2
    pair, u = gx // 2, gx % 2

    loads = [
        pltpu.make_async_copy(src, dst, load_sem.at[i])
        for i, (src, dst) in enumerate(
            [
                (order_h, order), (rs_h, rs), (basis_h, basis), (t_h, tr), (bt_h, bt),
                (lcp_h, lcp), (bcp_h, bcp), (ccp_h, ccp),
            ]
        )
    ]
    near_loads = [
        pltpu.make_async_copy(near_h.at[i // 4, i % 4], near.at[i], near_sem.at[i])
        for i in range(8)
    ]
    for copy in loads[:5]:
        copy.start()

    barrier = pltpu.get_barrier_semaphore()

    def tell(to_gx, to_gy):
        pl.semaphore_signal(barrier, inc=1, device_id=(to_gx, to_gy), device_id_type=MESH)

    own = z * 2 + c
    flip = z + 1 - 2 * (z % 2)
    half_id = z % 2
    keeps = y // 2 == half_id
    far_first = sorted(range(1, 16), key=lambda d: abs(d - 8))
    for d in far_first:
        t = (own + d) % 16
        tell(8 * y + t // 2, 2 * x + t % 2)
    for dx in (2, 1, 3, 0):
        for j in range(2):
            from_y = 2 * half_id + (y + j) % 2
            from_z = z if j == 0 else flip
            from_x = (x + 4 - dx) % 4
            if j == 0 and dx == 0:

                @pl.when(jnp.logical_not(keeps))
                def _():
                    tell(8 * from_y + from_z, 2 * from_x + c)
            else:
                tell(8 * from_y + from_z, 2 * from_x + c)
    left, right = (gy + 7) % 8, (gy + 1) % 8
    up, down = (gx + 31) % 32, (gx + 1) % 32
    partner = 2 * pair + 1 - u
    targets = []
    for step in (-1, 1, 0):
        for ut in range(2):
            to_gx = partner if step == 0 else 2 * ((pair + 16 + step) % 16) + ut
            if step == 0 and ut == 1:
                continue
            for to_gy, column in ((left, 2), (gy, 1), (right, 0)):
                targets.append((step, to_gx, to_gy, column))
    targets += [(None, gx, left, 2), (None, gx, right, 0)]
    for _, to_gx, to_gy, _ in targets:
        tell(to_gx, to_gy)
    for copy in near_loads:
        copy.start()
    for copy in loads[5:]:
        copy.start()

    low8 = low_lanes((8, 128))
    low4 = low_lanes((4, 128))

    loads[0].wait()
    loads[1].wait()
    places = lax.broadcasted_iota(jnp.int32, (256, 256), 0)
    ordered = []
    for i in range(8):
        r, k = i // 4, i % 4
        chosen = (places == order[r, k : k + 1, :]).astype(F32).astype(BF16)
        sel[i] = chosen
        points = dot_nn(rs[r, k], chosen)
        ordered.append(points)
        ohalo[1 + r, 1 + k] = points.astype(BF16)
    loads[2].wait()
    tiles = {}
    for r in range(2):
        for w in range(2):
            both = jnp.concatenate([ordered[4 * r + 2 * w], ordered[4 * r + 2 * w + 1]], 0)
            out = dot_nt(both.astype(BF16), basis[r, 2 * w : 2 * w + 2].reshape(128, 256))
            tiles[r, w] = jnp.where(low8, out[:8], out[8:])
            lwin[2 + r, 1 + w] = tiles[r, w]
    loads[3].wait()
    for w in range(2):
        for r in range(2):
            for v in range(2):
                at = (2 * r + v) * 64
                tcat[at : at + 64, 64 * w : 64 * w + 64] = tr[r, 2 * w + v]
    stacked = [split(jnp.concatenate([tiles[0, w], tiles[1, w]], 1)) for w in range(2)]
    out = dot_nn(jnp.concatenate(stacked, 0), tcat[...])
    box = jnp.where(low8, joined(out, 0), joined(out, 16))
    bwin[2 + u, 1] = box
    loads[4].wait()
    bt_all = bt[0].reshape(128, 64)
    part = joined(dot_nn(split(box), jnp.concatenate([bt_all, bt_all], 1)))
    pack[own] = jnp.where(low4, part[:4], part[4:])

    pl.semaphore_wait(barrier, jnp.where(keeps, 39, 40))

    sends = []

    def send(src, dst, ssem, rsem, to):
        copy = pltpu.make_async_remote_copy(
            src, dst, ssem, rsem, device_id=to, device_id_type=MESH
        )
        copy.start()
        sends.append(copy)

    for n, d in enumerate(far_first):
        t = (own + d) % 16
        send(
            pack.at[own], pack.at[own], p1_send.at[n], p1_recv.at[z // 4],
            (8 * y + t // 2, 2 * x + t % 2),
        )
    mine, mid, cols = pl.ds(1, 2), pl.ds(2, 2), pl.ds(1, 4)
    above, below, pairs2 = pl.ds(0, 2), pl.ds(4, 2), pl.ds(1, 2)
    for n, (src, dst, rsem, to) in enumerate([
        (ohalo.at[2, cols], ohalo.at[0, cols], 0, (down, gy)),
        (ohalo.at[1, cols], ohalo.at[3, cols], 1, (up, gy)),
        (ohalo.at[2, 4], ohalo.at[0, 0], 0, (down, right)),
        (ohalo.at[2, 1], ohalo.at[0, 5], 0, (down, left)),
        (ohalo.at[1, 4], ohalo.at[3, 0], 1, (up, right)),
        (ohalo.at[1, 1], ohalo.at[3, 5], 1, (up, left)),
        (ohalo.at[mine, 4], ohalo.at[mine, 0], 2, (gx, right)),
        (ohalo.at[mine, 1], ohalo.at[mine, 5], 3, (gx, left)),
    ]):
        send(src, dst, o_send.at[n], o_recv.at[rsem], to)
    for n, (src, dst, rsem, to) in enumerate([
        (lwin.at[mid, pairs2], lwin.at[above, pairs2], 0, (down, gy)),
        (lwin.at[mid, pairs2], lwin.at[below, pairs2], 1, (up, gy)),
        (lwin.at[mid, 2], lwin.at[above, 0], 0, (down, right)),
        (lwin.at[mid, 1], lwin.at[above, 3], 0, (down, left)),
        (lwin.at[mid, 2], lwin.at[below, 0], 1, (up, right)),
        (lwin.at[mid, 1], lwin.at[below, 3], 1, (up, left)),
        (lwin.at[mid, 2], lwin.at[mid, 0], 2, (gx, right)),
        (lwin.at[mid, 1], lwin.at[mid, 3], 3, (gx, left)),
    ]):
        send(src, dst, l_send.at[n], l_recv.at[rsem], to)
    for n, (step, to_gx, to_gy, column) in enumerate(targets):
        slot = 2 + u if step is None else 2 - 2 * step + u
        send(
            bwin.at[2 + u, 1], bwin.at[slot, column], b_send.at[n], b_recv.at[slot],
            (to_gx, to_gy),
        )

    def near_terms(i, inside):
        r, k = i // 4, i % 4
        total = None
        for a in (-1, 0, 1):
            for b in (-1, 0, 1):
                if (0 <= r + a < 2 and 0 <= k + b < 4) != inside:
                    continue
                q = 3 * (a + 1) + b + 1
                term = dot_nt(
                    ohalo[1 + r + a, 1 + k + b], near[i, :, q * 256 : (q + 1) * 256]
                )
                total = term if total is None else total + term
        return total

    for r in range(2):
        for w in range(2):
            i = (2 * r + w) * 256
            down_two = dot_nn(tr[r, 2 * w : 2 * w + 2].reshape(128, 64), bt[0, w])
            down_high = down_two.astype(BF16)
            through[i : i + 128] = down_high
            through[i + 128 : i + 256] = (down_two - down_high.astype(F32)).astype(BF16)
    for i in range(8):
        near_loads[i].wait()
        acc[i] = near_terms(i, True)
        basis_in[i] = dot_nt(basis[i // 4, i % 4], sel[i]).astype(BF16)

    my_half = y // 2
    odd = jnp.where(z % 2 == my_half, 0, 1)
    to_z = z + odd * (1 - 2 * (z % 2))
    slot = (y % 2) * 4 + x
    stage2 = []
    for g in range(2):
        for others in (7, 8):

            @pl.when((z // 4 == g) == (others == 7))
            def _():
                arrived = pack.at[pl.ds(0, others)]
                pltpu.make_async_copy(arrived, arrived, p1_recv.at[g]).wait()

        for zp in (2 * g, 2 * g + 1):
            pairs = [pack[4 * zp + k] + pack[4 * zp + 2 + k] for k in range(2)]
            turned = [pltpu.roll(p, 64, 1) for p in pairs]
            row[zp] = jnp.concatenate(
                [jnp.where(low4, pairs[0], turned[1]), jnp.where(low4, turned[0], pairs[1])], 0
            )
        two = pl.ds(2 * g, 2)
        for i in range(2):
            for dx in (2, 1, 3, 0):
                to_y = (y + 2 * i + odd) % 4
                to_x = (x + dx) % 4
                copy = pltpu.make_async_remote_copy(
                    row.at[two], coarse.at[slot, two],
                    p2_send.at[len(stage2)], p2_recv.at[g],
                    device_id=(8 * to_y + to_z, 2 * to_x + c), device_id_type=MESH,
                )
                itself = i == 0 and dx == 0
                stage2.append((itself, copy))
                if itself:

                    @pl.when(odd == 1)
                    def _():
                        copy.start()

                    @pl.when(odd == 0)
                    def _():
                        pltpu.make_async_copy(
                            row.at[two], coarse.at[slot, two], p2_recv.at[g]
                        ).start()
                else:
                    copy.start()

    def arrive(ref, sem):
        pltpu.make_async_copy(ref, ref, sem).wait()

    arrive(ohalo.at[0], o_recv.at[0])
    arrive(ohalo.at[3], o_recv.at[1])
    arrive(ohalo.at[mine, 0], o_recv.at[2])
    arrive(ohalo.at[mine, 5], o_recv.at[3])
    arrive(lwin.at[above], l_recv.at[0])
    arrive(lwin.at[below], l_recv.at[1])
    arrive(lwin.at[mid, 0], l_recv.at[2])
    arrive(lwin.at[mid, 3], l_recv.at[3])
    for a in (0, 1, 4, 5):
        arrive(bwin.at[a], b_recv.at[a])
    arrive(bwin.at[3 - u], b_recv.at[3 - u])
    arrive(bwin.at[2 + u, pl.ds(0, 2)], b_recv.at[2 + u])

    @pl.when(gy == 0)
    def _():
        ohalo[:, 0] = jnp.zeros((4, 8, 256), BF16)
        lwin[:, 0] = jnp.zeros((6, 8, 128), F32)
        bwin[:, 0] = jnp.zeros((6, 8, 128), F32)

    @pl.when(gy == 7)
    def _():
        ohalo[:, 5] = jnp.zeros((4, 8, 256), BF16)
        lwin[:, 3] = jnp.zeros((6, 8, 128), F32)
        bwin[:, 2] = jnp.zeros((6, 8, 128), F32)

    @pl.when(gx == 0)
    def _():
        ohalo[0] = jnp.zeros((6, 8, 256), BF16)
        lwin[0:2] = jnp.zeros((2, 4, 8, 128), F32)

    @pl.when(gx == 31)
    def _():
        ohalo[3] = jnp.zeros((6, 8, 256), BF16)
        lwin[4:6] = jnp.zeros((2, 4, 8, 128), F32)

    @pl.when(pair == 0)
    def _():
        bwin[0:2] = jnp.zeros((2, 3, 8, 128), F32)

    @pl.when(pair == 15)
    def _():
        bwin[4:6] = jnp.zeros((2, 3, 8, 128), F32)

    for i in range(8):
        acc[i] += near_terms(i, False)

    loads[5].wait()
    leaf_tiles = [[lwin[a, j] for j in range(4)] for a in range(6)]
    leaf_turned = [[pltpu.roll(t, 64, 1) for t in line] for line in leaf_tiles]
    leaf_far = {}
    for r in range(2):
        for w in range(2):
            here = [line[w : w + 3] for line in leaf_tiles]
            here_turned = [line[w : w + 3] for line in leaf_turned]
            both = [
                split(jnp.concatenate(listed(here, here_turned, r, v, low8), 1))
                for v in range(2)
            ]
            out = dot_nt(
                jnp.concatenate(both, 0), lcp[r, 2 * w : 2 * w + 2].reshape(128, 1728)
            )
            leaf_far[r, w] = jnp.where(low8, joined(out, 0), joined(out, 16))
    loads[6].wait()
    box_tiles = [[bwin[a, j] for j in range(3)] for a in range(6)]
    box_turned = [[pltpu.roll(t, 64, 1) for t in line] for line in box_tiles]
    both = []
    for v in range(2):
        even = jnp.concatenate(listed(box_tiles, box_turned, 0, v, low8), 1)
        odds = jnp.concatenate(listed(box_tiles, box_turned, 1, v, low8), 1)
        both.append(split(jnp.where(u == 0, even, odds)))
    out = dot_nt(jnp.concatenate(both, 0), bcp[0].reshape(128, 1728))
    box_far = jnp.where(low8, joined(out, 0), joined(out, 16))

    for copy in sends:
        copy.wait_send()
    loads[7].wait()
    lane = lax.broadcasted_iota(jnp.int32, (8, 128), 1)
    near_cols = []
    for xs in range(4):
        apart = 2 * xs + lane // 64 - gy
        near_cols.append((apart >= -1) & (apart <= 1))
    here = None
    for g in range(2):
        arrive(coarse.at[pl.ds(0, 4)], p2_recv.at[g])
        for yb in range(2):
            sources = []
            for zp in (2 * g, 2 * g + 1):
                apart = 8 * half_id + 4 * yb + zp - pair
                near_row = (apart >= -1) & (apart <= 1)
                for xs in range(4):
                    sources.append(
                        jnp.where(near_cols[xs] & near_row, 0.0, coarse[4 * yb + xs, zp])
                    )
            first = (4 * yb + 2 * g) * 512
            term = dot_nt(
                split(jnp.concatenate(sources, 1)), ccp[0, 0, :, first : first + 1024]
            )
            here = term if here is None else here + term
    here = joined(here)
    half[...] = here
    swap = pltpu.make_async_remote_copy(
        half, other_half, x_send.at[0], x_recv.at[0], device_id=(partner, gy), device_id_type=MESH
    )
    swap.start()
    both = [split(jnp.where(low8, box_far, 0.0)), split(jnp.where(low8, 0.0, box_far))]
    out = dot_nt(jnp.concatenate(both, 0), tcat[...])
    for r in range(2):
        for w in range(2):
            leaf_far[r, w] += joined(out[:, 128 * r : 128 * r + 128], 16 * w)
    for i in range(8):
        acc[i] = joined(dot_nt(split(acc[i]), sel[i]))
    for itself, copy in stage2:
        if itself:

            @pl.when(odd == 1)
            def _():
                copy.wait_send()
        else:
            copy.wait_send()
    swap.wait()

    coarse_far = here + other_half[...]
    out = joined(dot_nt(split(coarse_far), through[...]))
    for r in range(2):
        for w in range(2):
            i = (2 * r + w) * 256
            leaf_down = out[:, i : i + 128] + out[:, i + 128 : i + 256] + leaf_far[r, w]
            both = [split(jnp.where(low8, leaf_down, 0.0)), split(jnp.where(low8, 0.0, leaf_down))]
            i = 4 * r + 2 * w
            last = dot_nn(jnp.concatenate(both, 0), basis_in[i : i + 2].reshape(128, 256))
            for v in range(2):
                out_ref[r, 2 * w + v] = joined(last, 16 * v) + acc[i + v]


def body(*args):
    rs, order, basis, _, lcp, tr, bcp, bt, ccp = args
    hbm = pl.BlockSpec(memory_space=pltpu.HBM)
    dma = pltpu.SemaphoreType.DMA
    return pl.pallas_call(
        kernel,
        out_shape=jax.ShapeDtypeStruct((2, 4, 8, 256), F32),
        in_specs=[hbm] * 9,
        out_specs=pl.BlockSpec(memory_space=pltpu.VMEM),
        scratch_shapes=[
            pltpu.VMEM(rs.shape, BF16),
            pltpu.VMEM(order.shape, jnp.int32),
            pltpu.VMEM(basis.shape, BF16),
            pltpu.VMEM((8, 256, 2304), BF16),
            pltpu.VMEM(lcp.shape, BF16),
            pltpu.VMEM(tr.shape, BF16),
            pltpu.VMEM(bcp.shape, BF16),
            pltpu.VMEM(bt.shape, BF16),
            pltpu.VMEM(ccp.shape, BF16),
            pltpu.VMEM((8, 256, 256), BF16),
            pltpu.VMEM((256, 128), BF16),
            pltpu.VMEM((4, 6, 8, 256), BF16),
            pltpu.VMEM((6, 4, 8, 128), F32),
            pltpu.VMEM((6, 3, 8, 128), F32),
            pltpu.VMEM((16, 4, 128), F32),
            pltpu.VMEM((4, 8, 128), F32),
            pltpu.VMEM((8, 4, 8, 128), F32),
            pltpu.VMEM((8, 64), F32),
            pltpu.VMEM((8, 64), F32),
            pltpu.VMEM((8, 8, 256), F32),
            pltpu.VMEM((8, 64, 256), BF16),
            pltpu.VMEM((1024, 64), BF16),
            dma((8,)),
            dma((8,)),
            dma((15,)),
            dma((2,)),
            dma((16,)),
            dma((2,)),
            dma((8,)),
            dma((4,)),
            dma((8,)),
            dma((4,)),
            dma((17,)),
            dma((6,)),
            dma((1,)),
            dma((1,)),
        ],
        compiler_params=pltpu.CompilerParams(
            collective_id=0, has_side_effects=True, vmem_limit_bytes=40 * 2**20
        ),
    )(*(pltpu.with_memory_space_constraint(v, pltpu.HBM) for v in args))


def solution(mesh):
    four = P("gx", "gy", None, None)
    placed = (four, P("gx", "gy", None)) + (four,) * 7
    return jax.shard_map(body, mesh=mesh, in_specs=placed, out_specs=four, check_vma=False)
```
